32 devices in a mesh: body: 2 (over core), gx: 4 (over z), gy: 4 (over y, x).
Axes of the slice: x: 2, y: 2, z: 4, core: 2. Of those that a mesh axis runs over, the one named last changes fastest.
Arguments:
- disp: float32 [2, 3, 32, 128, 128], P('body', None, 'gx', 'gy'), may hold values from -4 to 4
- force: float32 [2, 3, 32, 128, 128], P('body', None, 'gx', 'gy'), may hold values from -12 to 12
- kappa: float32 [2, 32, 128, 128], P('body', 'gx', 'gy'), may hold values from 0.05 to 0.5
- sigma: float32 [2, 32, 128, 128], P('body', 'gx', 'gy'), may hold values from 0.2 to 1
- gap0: float32 [32, 128], P(('gx', 'gy')), may hold values from -3 to 3
- pressure: float32 [32, 128], P(('gx', 'gy')), may hold values from 0 to 1
- mortar: float32 [32, 128, 128], P(('gx', 'gy')), may hold values from -0.5 to 0.5
- partner: int32 [32], P(('gx', 'gy')), may hold values from 0 to 7
- active: int32 [32], P(('gx', 'gy')), may hold values 0 or 1
Outputs:
- increment: float32 [2, 3, 32, 128, 128], P('body', None, 'gx', 'gy')
- new_pressure: float32 [32, 128], P(('gx', 'gy'))
The draws below stay inside these ranges and needn't reach their ends.
Inputs may be any that keep to these rules, and one draw needn't show every extreme that they name: partner numbers a master block of the same gy index: gx index times 2 plus the local block. 1 marks a block of the active contact set.
All inputs are finite; a program needn't handle non-finite values.
Results may differ from the reference program's by a relative error of at most 0.00015.
Values sent between devices are 32-bit elements; how exact they have to be, the bound alone decides.
A program may use at most 64 MiB of HBM per device.

```python
import math
import jax
import jax.numpy as jnp
from jax import lax

CX = 8
CY = 32
NZ = 128
SBLK = 128
COMP = 3
CG_ITERS = 2
BLK_DEV = 2
ROWBLK = 8
NBLK = 32
NX = 32
NY = 128
N_GX = 4
N_GY = 4


def plant(values, rng, low, top_value):
    longest = values.shape.index(max(values.shape))
    spots = []
    for shift in (0, 1):
        where = [jax.random.randint(jax.random.fold_in(rng, axis), (), 0, length) for axis, length in enumerate(values.shape)]
        where[longest] = (where[longest] + shift) % values.shape[longest]
        spots.append(tuple(where))
    return values.at[spots[0]].set(low).at[spots[1]].set(top_value)


def level_of(own_key, extent, pieces, low, top_value):
    factor_of = 1.0
    for axis_at, parts in pieces:
        draws = jax.random.uniform(jax.random.fold_in(jax.random.fold_in(own_key, 6), axis_at), (parts,), jnp.float32, low / len(pieces), top_value / len(pieces))
        factor_of = factor_of * jnp.repeat(jnp.exp(draws), extent[axis_at] // parts).reshape((-1,) + (1,) * (len(extent) - 1 - axis_at))
    return factor_of


def scatter_about(stream_key, dims, scale, most, cuts=(), kind=jnp.bfloat16):
    entries = jax.random.normal(stream_key, dims, jnp.float32) * scale
    if len(cuts) > 0:
        entries = level_of(stream_key, dims, cuts, -0.22, 0.18) * entries
    return jnp.clip(entries, min=-most, max=most).astype(kind)


def setup_inputs(seed: int = 0) -> dict:
    streams_of = jax.random.split(jax.random.key(seed), 10)
    return {
        "disp": scatter_about(streams_of[0], (2, COMP, NX, NY, NZ), 0.5, 4.0, ((0, 2), (2, 4), (3, 4)), jnp.float32),
        "force": scatter_about(streams_of[1], (2, COMP, NX, NY, NZ), 2.0, 12.0, ((0, 2), (2, 4), (3, 4)), jnp.float32),
        "kappa": jnp.clip(jnp.exp(math.log(0.5) - 2.3025851 * jax.random.uniform(streams_of[2], (2, NX, NY, NZ), jnp.float32) ** level_of(streams_of[2], (2, NX, NY, NZ), ((0, 2), (1, 4), (2, 4)), -0.2, 0.2)), 0.05, 0.5),
        "sigma": jnp.clip(jnp.exp(math.log(1.0) - 1.609438 * jax.random.uniform(streams_of[3], (2, NX, NY, NZ), jnp.float32) ** level_of(streams_of[3], (2, NX, NY, NZ), ((0, 2), (1, 4), (2, 4)), -0.2, 0.2)), 0.2, 1.0),
        "gap0": scatter_about(streams_of[4], (NBLK, SBLK), 0.5, 3.0, ((0, 16),), jnp.float32),
        "pressure": jnp.clip(1.0 * jax.random.uniform(streams_of[5], (NBLK, SBLK), jnp.float32) ** level_of(streams_of[5], (NBLK, SBLK), ((0, 16),), -0.2, 0.2), 0.0, 1.0),
        "mortar": scatter_about(streams_of[6], (NBLK, SBLK, SBLK), SBLK ** -0.5, 0.5, ((0, 16),), jnp.float32),
        "partner": plant(jax.random.randint(streams_of[7], (NBLK,), 0, ROWBLK), jax.random.fold_in(streams_of[7], 1), 0, ROWBLK - 1).astype(jnp.int32),
        "active": plant((jax.random.randint(streams_of[8], (NBLK,), 0, 2) < 1).astype(jnp.int32), jax.random.fold_in(streams_of[8], 1), 0, 1),
    }


def neighbours():
    result = []
    for first in (-1, 0, 1):
        for second in (-1, 0, 1):
            for third in (-1, 0, 1):
                if first != 0 or second != 0 or third != 0:
                    result.append((first, second, third))
    return result

def apply_stencil(field, padded, kappa, kappa_rim, sigma):
    sizes = field.shape[2:]
    total = sigma[:, None] * field
    for offset in neighbours():
        weight = 0.5 ** (abs(offset[0]) + abs(offset[1]) + abs(offset[2]) - 1)
        lower = [1 + offset[0], 1 + offset[1], 1 + offset[2]]
        bond = 0.5 * (kappa + kappa_rim[:, lower[0]:lower[0] + sizes[0], lower[1]:lower[1] + sizes[1], lower[2]:lower[2] + sizes[2]])
        near = padded[:, :, lower[0]:lower[0] + sizes[0], lower[1]:lower[1] + sizes[1], lower[2]:lower[2] + sizes[2]]
        total = total + weight * bond[:, None] * (field - near)
    return total

def stencil(field, kappa, sigma):
    padded = jnp.pad(field, ((0, 0), (0, 0), (1, 1), (1, 1), (1, 1)))
    kappa_rim = jnp.pad(kappa, ((0, 0), (1, 1), (1, 1), (1, 1)))
    return apply_stencil(field, padded, kappa, kappa_rim, sigma)

def blocks_of(field):
    surface = field[:, 2, :, :, 0]
    surface = surface.reshape(2, N_GX, CX, N_GY, CY).transpose(0, 1, 3, 2, 4)
    return surface.reshape(2, N_GX, N_GY, BLK_DEV, SBLK)

def gap_of(field, partner_grid, mortar_grid):
    surfaces = blocks_of(field)
    master_row = surfaces[1].transpose(1, 0, 2, 3).reshape(N_GY, N_GX * BLK_DEV, SBLK)
    row_index = jnp.arange(N_GY, dtype=jnp.int32)[None, :, None]
    picked = master_row[row_index, partner_grid]
    pulled = jnp.einsum('abcij,abcj->abci', mortar_grid, picked, precision=lax.Precision.HIGHEST)
    return -surfaces[0] - pulled

def spread(traction, partner_grid, mortar_grid):
    pulled = jnp.einsum('abcij,abci->abcj', mortar_grid, traction, precision=lax.Precision.HIGHEST)
    row_index = jnp.arange(N_GY, dtype=jnp.int32)[None, :, None]
    master_row = jnp.zeros((N_GY, N_GX * BLK_DEV, SBLK), jnp.float32).at[row_index, partner_grid].add(-pulled)
    master = master_row.reshape(N_GY, N_GX, BLK_DEV, SBLK).transpose(1, 0, 2, 3)
    both = jnp.stack([-traction, master])
    both = both.reshape(2, N_GX, N_GY, CX, CY).transpose(0, 1, 3, 2, 4)
    return both.reshape(2, NX, NY)

def reference(disp, force, kappa, sigma, gap0, pressure, mortar, partner, active):
    mortar_grid = mortar.reshape(N_GX, N_GY, BLK_DEV, SBLK, SBLK)
    partner_grid = partner.reshape(N_GX, N_GY, BLK_DEV).astype(jnp.int32)
    press = pressure.reshape(N_GX, N_GY, BLK_DEV, SBLK)
    flags = active.reshape(N_GX, N_GY, BLK_DEV, 1).astype(jnp.float32)
    gap = gap0.reshape(N_GX, N_GY, BLK_DEV, SBLK) + gap_of(disp, partner_grid, mortar_grid)
    radius = jnp.sqrt(gap * gap + press * press + 0.01)
    complement = gap + press - radius
    slope_gap = 1.0 - gap / radius
    slope_press = 1.0 - press / radius
    divisor = slope_press + 0.5
    stiffness = flags * slope_gap / divisor
    excess = flags * complement / divisor
    rhs = force - stencil(disp, kappa, sigma)
    rhs = rhs.at[:, 2, :, :, 0].add(spread(flags * press - excess, partner_grid, mortar_grid))

    def operate(field):
        image = stencil(field, kappa, sigma)
        return image.at[:, 2, :, :, 0].add(spread(stiffness * gap_of(field, partner_grid, mortar_grid), partner_grid, mortar_grid))
    increment = jnp.zeros_like(rhs)
    residual, direction = (rhs, rhs)
    norm_now = jnp.sum(residual * residual)
    for step in range(CG_ITERS):
        image = operate(direction)
        alpha = norm_now / jnp.sum(direction * image)
        increment = increment + alpha * direction
        residual = residual - alpha * image
        norm_next = jnp.sum(residual * residual)
        direction = residual + norm_next / norm_now * direction
        norm_now = norm_next
    change = gap_of(increment, partner_grid, mortar_grid)
    new_press = flags * (press - (complement + slope_gap * change) / divisor)
    return (increment, new_press.reshape(NBLK, SBLK))
```

```python
import functools

import jax
import jax.numpy as jnp
from jax import lax
from jax.experimental import pallas as pl
from jax.experimental.pallas import tpu as pltpu
from jax.sharding import PartitionSpec as P

MESH = pl.DeviceIdType.MESH
YB = 8
CORNERS = tuple((dx, dy) for dx in (-1, 1) for dy in (-1, 1))
DIRS = CORNERS + ((0, -1), (0, 1), (-1, 0), (1, 0))
RR, RV, VV, NN, NV, NW, VW, OWN = range(8)


def kernel(nb, ngx, ngy, disp, force, kappa, sigma, gap0_in, press_in, mortar, partner_in, active_in,
           r0_out, v1_out, coef, npr_out,
           gap0, press, partner, active, f0, f1, f2, npr, diag, force_v, sigma_v, mort, s1b, pbuf, ub, base, prs_f, t_f, ex_f, sl_f,
           st_f, gr_f, gv_f, acc, own_ref, final, dummy,
           ls, hr, hs, sr, ss, pr, pn, ps, nps, fin):
    comp, cx, cy, nz = force_v.shape
    bpd, sblk = gap0.shape
    per = sblk // cy
    rowblk = ngx * bpd
    last = comp - 1
    b = lax.axis_index("body")
    gx = lax.axis_index("gx")
    gy = lax.axis_index("gy")
    count = nb * ngx * ngy
    me = (b * ngx + gx) * ngy + gy
    f32 = jnp.float32

    def far(at, k, size):
        if size & (size - 1):
            return lax.rem(at + k, size)
        for bit in (1 << i for i in range(size.bit_length() - 1)):
            if k & bit:
                at = at + bit - 2 * bit * lax.rem(at // bit, 2)
        return at

    def place_of(other):
        return {"body": other // (ngx * ngy), "gx": lax.rem(other // ngy, ngx), "gy": lax.rem(other, ngy)}

    def each_peer(act):
        if count <= 64:
            for k in range(1, count):
                act(k)
        else:
            pl.loop(1, count)(act)

    def exists(dx, dy):
        good = jnp.bool_(True)
        if dx < 0:
            good = good & (gx >= 1)
        if dx > 0:
            good = good & (gx < ngx - 1)
        if dy < 0:
            good = good & (gy >= 1)
        if dy > 0:
            good = good & (gy < ngy - 1)
        return good

    def as_int(flag):
        return flag.astype(jnp.int32)

    nys = as_int(exists(0, -1)) + as_int(exists(0, 1))
    nxs = as_int(exists(-1, 0)) + as_int(exists(1, 0))

    def sides(size):
        return (0,) if size == 1 else (1,) if size == 2 else (1, 2)

    def wait_rows(sem, rows):
        part = dummy.at[pl.ds(0, rows)]
        pltpu.make_async_copy(part, part, sem).wait()

    def wait_halo(sem, comps):
        for a in sides(ngx):
            for c in sides(ngy):
                rows = comps * (a * cy + c * cx + a * c)
                if rows:
                    pl.when((nxs == a) & (nys == c))(lambda: wait_rows(sem, rows))

    barrier = pltpu.get_barrier_semaphore()
    if ngy <= 4:
        expect = jnp.where(b == 1, ngx, 0)
        for dx, dy in DIRS:
            here = exists(dx, dy)
            expect = expect + as_int(here)

            @pl.when(here)
            def _():
                pl.semaphore_signal(barrier, inc=1, device_id={"gx": gx + dx, "gy": gy + dy}, device_id_type=MESH)
        for g in range(ngx):
            @pl.when(b == 0)
            def _():
                pl.semaphore_signal(barrier, inc=1, device_id={"body": 1, "gx": g}, device_id_type=MESH)
    else:
        each_peer(lambda k: pl.semaphore_signal(barrier, inc=1, device_id=place_of(lax.rem(me + k, count)),
                                                device_id_type=MESH))
        expect = count - 1

    inner = (pl.ds(1, cx), pl.ds(YB, cy))
    pltpu.make_async_copy(disp.at[0, last], f0.at[(last,) + inner], ls.at[0]).start()
    pltpu.make_async_copy(disp.at[0, pl.ds(0, last)], f0.at[(pl.ds(0, last),) + inner], ls.at[1]).start()
    pltpu.make_async_copy(kappa.at[0], f0.at[(comp,) + inner], ls.at[1]).start()
    pltpu.make_async_copy(gap0_in, gap0, ls.at[3]).start()
    pltpu.make_async_copy(press_in, press, ls.at[3]).start()
    pltpu.make_async_copy(partner_in, partner, ls.at[4]).start()
    pltpu.make_async_copy(active_in, active, ls.at[5]).start()
    pltpu.make_async_copy(mortar, mort, ls.at[6]).start()
    pltpu.make_async_copy(sigma.at[0], sigma_v, ls.at[2]).start()
    pltpu.make_async_copy(force.at[0], force_v, ls.at[2]).start()

    for side, x in ((-1, 0), (1, cx + 1)):
        @pl.when(jnp.logical_not(exists(side, 0)))
        def _():
            for f in (f0, f1, f2):
                for c in range(f.shape[0]):
                    f[c, x, YB - 1 : YB] = jnp.zeros((1, nz), f32)
                    f[c, x, YB : YB + cy] = jnp.zeros((cy, nz), f32)
                    f[c, x, YB + cy : YB + cy + 1] = jnp.zeros((1, nz), f32)
    for side, y in ((-1, YB - 1), (1, YB + cy)):
        @pl.when(jnp.logical_not(exists(0, side)))
        def _():
            for f in (f0, f1, f2):
                for c in range(f.shape[0]):
                    for x in range(cx + 2):
                        f[c, x, y : y + 1] = jnp.zeros((1, nz), f32)
            for g in range(ngx):
                for k in range(3):
                    for l in range(bpd):
                        pbuf[1 + side, g, k, l] = jnp.zeros((1, sblk), f32)
    for d in range(3):
        for q in (0, rowblk + 1):
            ub[d, q] = jnp.zeros((1, sblk), f32)
    for k in range(8):
        acc[k] = jnp.zeros((8, nz), f32)

    lane = lax.broadcasted_iota(jnp.int32, (sblk, nz), 1)
    eye = lax.broadcasted_iota(jnp.int32, (sblk, nz), 0) == lane
    first_lane = lane == 0
    lane_row = lax.broadcasted_iota(jnp.int32, (cy, nz), 1)
    left_w = jnp.where(lane_row == 0, 0.0, 0.5)
    right_w = jnp.where(lane_row == nz - 1, 0.0, 0.5)
    lane_one = lax.broadcasted_iota(jnp.int32, (1, nz), 1)
    block_of = lax.broadcasted_iota(jnp.int32, (rowblk, sblk), 0)
    block_f = block_of.astype(f32)

    def to_full(row):
        return jnp.broadcast_to(jnp.sum(jnp.where(eye, row, 0.0), axis=1, keepdims=True), (sblk, nz))

    def to_row(full):
        return jnp.sum(jnp.where(eye, full, 0.0), axis=0, keepdims=True)

    def tz(v):
        return v + left_w * pltpu.roll(v, 1, 1) + right_w * pltpu.roll(v, nz - 1, 1)

    def block(f, l):
        return f[last, 1 + l * per : 1 + (l + 1) * per, YB : YB + cy, :].reshape(sblk, nz)

    def first_of(f, l):
        return jnp.broadcast_to(block(f, l)[:, 0:1], (sblk, nz))

    def take_off(f, l, full):
        xs = slice(1 + l * per, 1 + (l + 1) * per)
        f[last, xs, YB : YB + cy, :] = (block(f, l) - jnp.where(first_lane, full, 0.0)).reshape(per, cy, nz)

    def part(delta, size, base_at, src_base):
        if delta == 0:
            return pl.ds(src_base, size), pl.ds(base_at, size)
        if delta < 0:
            return pl.ds(src_base, 1), pl.ds(base_at + size, 1)
        return pl.ds(src_base + size - 1, 1), pl.ds(base_at - 1, 1)

    def halo_send(f, at, size, send_sem, recv_sem):
        cs = pl.ds(at, size)
        for dx, dy in DIRS:
            @pl.when(exists(dx, dy))
            def _():
                sx, tx = part(dx, cx, 1, 1)
                sy, ty = part(dy, cy, YB, YB)
                pltpu.make_async_remote_copy(
                    src_ref=f.at[cs, sx, sy], dst_ref=f.at[cs, tx, ty], send_sem=send_sem, recv_sem=recv_sem,
                    device_id={"gx": gx + dx, "gy": gy + dy}, device_id_type=MESH).start()

    def halo_send_args():
        for dx, dy in DIRS:
            @pl.when(exists(dx, dy))
            def _():
                sx, tx = part(dx, cx, 1, 0)
                sy, ty = part(dy, cy, YB, 0)
                for src, dst in ((disp.at[0, :, sx, sy], f0.at[pl.ds(0, comp), tx, ty]),
                                 (kappa.at[:, sx, sy], f0.at[pl.ds(comp, 1), tx, ty])):
                    pltpu.make_async_remote_copy(
                        src_ref=src, dst_ref=dst, send_sem=hs.at[0], recv_sem=hr.at[0],
                        device_id={"gx": gx + dx, "gy": gy + dy}, device_id_type=MESH).start()

    def surf_send(r):
        for k in reversed(range(ngx)):
            pltpu.make_async_remote_copy(
                src_ref=s1b.at[r, gx], dst_ref=s1b.at[r, gx], send_sem=ss.at[0], recv_sem=sr.at[r],
                device_id={"body": 0, "gx": far(gx, k, ngx)}, device_id_type=MESH).start()

    def surface_rows(f, r):
        for l in range(bpd):
            s1b[r, gx, l] = to_row(first_of(f, l))

    def pulled_send(first, size, recv_sem):
        ks = pl.ds(first, size)

        def go(bo, g):
            pltpu.make_async_remote_copy(
                src_ref=pbuf.at[1, gx, ks], dst_ref=pbuf.at[1, gx, ks], send_sem=ps.at[0], recv_sem=recv_sem,
                device_id={"body": bo, "gx": g}, device_id_type=MESH).start()
        for k in reversed(range(ngx)):
            go(1, far(gx, k, ngx))
            if k:
                go(0, far(gx, k, ngx))

    def pass_on(r, first, size):
        ks = pl.ds(first, size)
        for s in (-1, 1):
            @pl.when(exists(0, s))
            def _():
                pltpu.make_async_remote_copy(
                    src_ref=pbuf.at[1, :, ks], dst_ref=pbuf.at[1 - s, :, ks], send_sem=ps.at[0],
                    recv_sem=pn.at[r, (1 - s) // 2], device_id={"gy": gy + s}, device_id_type=MESH).start()

    def expand(d, k):
        u = jnp.zeros((rowblk, sblk), f32)
        for g in range(ngx):
            for l in range(bpd):
                u = u + jnp.where(block_f == pbuf[d, g, 1, l], pbuf[d, g, k, l], 0.0)
        return u

    def ring_fix(f, r, k, size):
        wait_rows(pr.at[r], ngx * size * bpd)
        pass_on(r, k, size)
        ub[1, 1 : 1 + rowblk] = expand(1, k).reshape(rowblk, 1, sblk)

        def row(d, j):
            return ub[d, gx * bpd + j]

        for l in range(bpd):
            take_off(f, l, to_full(row(1, 1 + l)))
        for j, x, at in ((0, 0, sblk - cy), (bpd + 1, cx + 1, 0)):
            col = jnp.sum(jnp.where(eye[at : at + cy], row(1, j), 0.0), axis=1, keepdims=True)
            f[last, x, YB : YB + cy, :] = f[last, x, YB : YB + cy, :] - jnp.where(lane_row == 0, col, 0.0)
        for d, y, off in ((0, YB - 1, cy - 1), (2, YB + cy, 0)):
            pl.when(exists(0, d - 1))(lambda: wait_rows(pn.at[r, d // 2], ngx * size * bpd))
            ub[d, 1 : 1 + rowblk] = expand(d, k).reshape(rowblk, 1, sblk)
            for xi in range(cx + 2):
                j = (xi - 1 + per) // per
                at = ((xi - 1 + per) % per) * cy + off
                val = pltpu.roll(row(d, j), (nz - at) % nz, 1)
                f[last, xi, y : y + 1, :] = f[last, xi, y : y + 1, :] - jnp.where(lane_one == 0, val, 0.0)

    def apply(f, c, emit):
        window = []
        for x in range(cx + 2):
            kap = [f0[comp, x, YB + s : YB + s + cy, :] for s in (-1, 0, 1)]
            val = [f[c, x, YB + s : YB + s + cy, :] for s in (-1, 0, 1)]
            window.append((val[1] + 0.5 * (val[0] + val[2]),
                           kap[1] * val[1] + 0.5 * (kap[0] * val[0] + kap[2] * val[2])))
            if x >= 2:
                p = window[x - 1][0] + 0.5 * (window[x - 2][0] + window[x][0])
                q = window[x - 1][1] + 0.5 * (window[x - 2][1] + window[x][1])
                k0 = f0[comp, x - 1, YB : YB + cy, :]
                v0 = f[c, x - 1, YB : YB + cy, :]
                emit(c, x - 2, diag[x - 2] * v0 - k0 * tz(p) - tz(q))

    def make_diag():
        window = []
        for x in range(cx + 2):
            kap = [f0[comp, x, YB + s : YB + s + cy, :] for s in (-1, 0, 1)]
            window.append(kap[1] + 0.5 * (kap[0] + kap[2]))
            if x >= 2:
                p = window[x - 1] + 0.5 * (window[x - 2] + window[x])
                diag[x - 2] = sigma_v[x - 2] + 8.0 * f0[comp, x - 1, YB : YB + cy, :] + tz(p)

    def emit_rhs(c, x, val):
        f1[c, 1 + x, YB : YB + cy, :] = force_v[c, x] - val

    def emit_v1(c, x, val):
        f2[c, 1 + x, YB : YB + cy, :] = val

    def r0_of(c, x):
        return f1[c, 1 + x, YB : YB + cy, :]

    def v1_of(c, x):
        return f2[c, 1 + x, YB : YB + cy, :]

    def fold(v):
        return jnp.sum(v.reshape(cy // 8, 8, nz), axis=0)

    def gather(c, wanted, fields):
        sums = {}
        for x in range(cx):
            for k, (left, right) in wanted.items():
                term = fold(fields(x)[left] * fields(x)[right])
                sums[k] = sums[k] + term if k in sums else term
        for k, v in sums.items():
            acc[k] = acc[k] + v

    def dots(c):
        gather(c, {RR: (0, 0), RV: (0, 1), VV: (1, 1)}, lambda x: (r0_of(c, x), v1_of(c, x)))

    def total(v):
        return jnp.sum(jnp.sum(v, axis=0, keepdims=True), axis=1, keepdims=True)

    def choose_own():
        rv, vv = total(acc[RV]), total(acc[VV])
        own = jnp.where(vv > 0.0, rv / jnp.where(vv > 0.0, vv, 1.0), 0.0)
        own_ref[...] = jnp.broadcast_to(own, (cy, nz))

    def near_dots(c):
        own = own_ref[...]
        gather(c, {NN: (0, 0), NV: (0, 1)}, lambda x: (r0_of(c, x) - own * v1_of(c, x), v1_of(c, x)))

    def image_dots(c, more):
        own = own_ref[...]
        sums = {}

        def emit(c, x, val):
            v = v1_of(c, x)
            r = r0_of(c, x)
            near = r - own * v
            terms = {NW: near * val, VW: v * val}
            if more:
                terms.update({RV: r * v, VV: v * v, NN: near * near, NV: near * v})
            for k, t in terms.items():
                sums[k] = sums[k] + fold(t) if k in sums else fold(t)
        apply(f2, c, emit)
        for k, v in sums.items():
            acc[k] = acc[k] + v

    def first_comps(act):
        @pl.loop(0, last)
        def _(c):
            act(c)

    def gap_of(l, s1):
        picked = jnp.sum(jnp.where(block_of == partner[l], s1, 0.0), axis=0, keepdims=True)
        return base[l] - jnp.broadcast_to(jnp.sum(mort[l] * picked, axis=1, keepdims=True), (sblk, nz))

    def pull(l, k, t):
        pbuf[1, gx, k, l] = jnp.sum(mort[l] * t, axis=0, keepdims=True)

    def surf_rows(r):
        return s1b[r].reshape(rowblk, sblk)

    def send_final():
        sub = lax.broadcasted_iota(jnp.int32, (8, nz), 0)
        stack = jnp.zeros((8, nz), f32)
        for k in range(OWN):
            stack = jnp.where(sub == k, jnp.broadcast_to(jnp.sum(acc[k], axis=0, keepdims=True), (8, nz)), stack)
        lanes = lax.broadcasted_iota(jnp.int32, (8, nz), 1)
        stack = jnp.where((sub == OWN) & (lanes == 0), own_ref[0:8, :], stack)
        final[me] = jnp.sum(jnp.where(sub == lanes, jnp.sum(stack, axis=1, keepdims=True), 0.0), axis=0, keepdims=True)

        def go(place):
            pltpu.make_async_remote_copy(
                src_ref=final.at[me], dst_ref=final.at[me], send_sem=fin.at[0], recv_sem=fin.at[1],
                device_id=place, device_id_type=MESH).start()
        if count <= 64:
            for kx in reversed(range(ngx)):
                for ky in reversed(range(ngy)):
                    for kb in reversed(range(nb)):
                        if kx or ky or kb:
                            go({"body": far(b, kb, nb), "gx": far(gx, kx, ngx), "gy": far(gy, ky, ngy)})
        else:
            each_peer(lambda k: go(place_of(lax.rem(me + k, count))))

    pl.semaphore_wait(barrier, expect)

    @pl.when(b == 1)
    def _():
        wait_rows(ls.at[0], cx * cy)
        surface_rows(f0, 0)
        surf_send(0)

    halo_send_args()

    @pl.when(b == 1)
    def _():
        wait_rows(ls.at[1], comp * cx * cy)
        wait_rows(ls.at[2], (comp + 1) * cx * cy)
        wait_halo(hr.at[0], comp + 1)
        make_diag()
        apply(f0, last, emit_rhs)
        surface_rows(f1, 1)
        surf_send(1)
        halo_send(f1, last, 1, hs.at[1], hr.at[2])
        first_comps(lambda c: apply(f0, c, emit_rhs))
        halo_send(f1, 0, last, hs.at[0], hr.at[1])

        wait_halo(hr.at[1], last)
        first_comps(lambda c: apply(f1, c, emit_v1))
        halo_send(f2, 0, last, hs.at[0], hr.at[3])
        first_comps(dots)
        choose_own()
        first_comps(near_dots)
        wait_halo(hs.at[1], 1)
        wait_halo(hr.at[2], 1)
        ring_fix(f1, 0, 0, 2)
        apply(f1, last, emit_v1)
        surface_rows(f2, 2)
        surf_send(2)
        halo_send(f2, last, 1, hs.at[2], hr.at[4])
        gather(last, {RR: (0, 0)}, lambda x: (r0_of(last, x),))

        wait_halo(hr.at[3], last)
        first_comps(lambda c: image_dots(c, False))
        wait_halo(hs.at[2], 1)
        wait_halo(hr.at[4], 1)
        ring_fix(f2, 1, 2, 1)
        image_dots(last, True)
        send_final()

    @pl.when(b == 0)
    def _():
        for k in range(4):
            sem, rows = ((ls.at[0], cx * cy), (ls.at[3], 2 * bpd), (ls.at[6], bpd * sblk), (ls.at[1], comp * cx * cy))[k]
            wait_rows(sem, rows)
        pltpu.make_async_copy(partner_in, partner, ls.at[4]).wait()
        pltpu.make_async_copy(active_in, active, ls.at[5]).wait()
        for l in range(bpd):
            base[l] = to_full(gap0[l : l + 1, :]) - first_of(f0, l)
            prs_f[l] = to_full(press[l : l + 1, :])
            pbuf[1, gx, 1, l] = jnp.full((1, sblk), partner[l].astype(f32))
        wait_rows(sr.at[0], ngx * bpd)
        s1 = surf_rows(0)
        for l in range(bpd):
            gap = gap_of(l, s1)
            prs = prs_f[l]
            radius = jnp.sqrt(gap * gap + prs * prs + 0.01)
            per_radius = 1.0 / radius
            per_divisor = 1.0 / ((1.0 - prs * per_radius) + 0.5)
            flag = active[l].astype(f32)
            excess = (gap + prs - radius) * per_divisor
            slope = (1.0 - gap * per_radius) * per_divisor
            t = flag * (prs - excess)
            pull(l, 0, t)
            t_f[l] = t
            ex_f[l] = excess
            sl_f[l] = slope
            st_f[l] = flag * slope
        pulled_send(0, 2, pr.at[0])
        wait_rows(ls.at[2], (comp + 1) * cx * cy)
        wait_halo(hr.at[0], comp + 1)
        make_diag()
        first_comps(lambda c: apply(f0, c, emit_rhs))
        halo_send(f1, 0, last, hs.at[0], hr.at[1])
        apply(f0, last, emit_rhs)
        for l in range(bpd):
            take_off(f1, l, t_f[l])
        halo_send(f1, last, 1, hs.at[1], hr.at[2])
        for l in range(bpd):
            base[l] = -first_of(f1, l)

        wait_rows(sr.at[1], ngx * bpd)
        if ngx > 1:
            wait_rows(pr.at[0], (ngx - 1) * 2 * bpd)
        s1 = surf_rows(1) - expand(1, 0)
        for l in range(bpd):
            gap = gap_of(l, s1)
            t = st_f[l] * gap
            pull(l, 2, t)
            t_f[l] = t
            gr_f[l] = gap
        pulled_send(2, 1, pr.at[1])
        wait_halo(hr.at[1], last)
        first_comps(lambda c: apply(f1, c, emit_v1))
        halo_send(f2, 0, last, hs.at[0], hr.at[3])
        wait_halo(hr.at[2], 1)
        apply(f1, last, emit_v1)
        for l in range(bpd):
            take_off(f2, l, t_f[l])
        halo_send(f2, last, 1, hs.at[2], hr.at[4])
        for l in range(bpd):
            base[l] = -first_of(f2, l)
        first_comps(dots)
        choose_own()
        dots(last)
        pl.loop(0, comp)(near_dots)
        wait_halo(hr.at[3], last)
        wait_halo(hr.at[4], 1)
        pl.loop(0, comp)(lambda c: image_dots(c, False))

        wait_rows(sr.at[2], ngx * bpd)
        if ngx > 1:
            wait_rows(pr.at[1], (ngx - 1) * bpd)
        s1 = surf_rows(2) - expand(1, 2)
        own = own_ref[0:1, :]
        for l in range(bpd):
            gap = gap_of(l, s1)
            gv_f[l] = gap
            weighted = st_f[l] * gap
            for k, left in ((NW, gr_f[l] - own * gap), (VW, gap)):
                row = jnp.sum(weighted * left, axis=0, keepdims=True)
                acc[k, 0:1] = acc[k, 0:1] + jnp.where(lane_one == 0, row, 0.0)
        send_final()
        for l in range(bpd):
            flag = active[l].astype(f32)
            npr[0, l] = flag * (press[l : l + 1, :] - to_row(ex_f[l]))
            npr[1, l] = flag * to_row(sl_f[l] * gr_f[l])
            npr[2, l] = flag * to_row(sl_f[l] * gv_f[l])
        pltpu.make_async_remote_copy(src_ref=npr, dst_ref=npr, send_sem=nps.at[0], recv_sem=nps.at[1],
                                     device_id={"body": 1}, device_id_type=MESH).start()

    @pl.when(b == 1)
    def _():
        wait_rows(ls.at[3], 2 * bpd)
        wait_rows(ls.at[6], bpd * sblk)
        pltpu.make_async_copy(partner_in, partner, ls.at[4]).wait()
        pltpu.make_async_copy(active_in, active, ls.at[5]).wait()
        wait_rows(ss.at[0], 3 * ngx * bpd)
        for c in sides(ngy):
            if c:
                pl.when(nys == c)(lambda: wait_rows(ps.at[0], 3 * bpd * c * ngx))
        wait_rows(nps.at[1], 3 * bpd)

    @pl.when(b == 0)
    def _():
        wait_rows(ps.at[0], 3 * bpd * (2 * ngx - 1))
        wait_halo(hs.at[1], 1)
        wait_halo(hs.at[2], 1)
        wait_rows(nps.at[0], 3 * bpd)

    wait_halo(hs.at[0], comp + 1 + 2 * last)
    wait_rows(fin.at[0], count - 1)
    for c in range(comp):
        for x in range(cx):
            r0_out[c, x] = r0_of(c, x)
            v1_out[c, x] = v1_of(c, x)
    npr_out[...] = npr[...]

    wait_rows(fin.at[1], count - 1)
    table = final[...].reshape(count, sblk)
    lanes = lax.broadcasted_iota(jnp.int32, (count, sblk), 1)
    sums = jnp.sum(table, axis=0, keepdims=True)
    norm0 = sums[:, RR : RR + 1]
    alpha0 = norm0 / sums[:, RV : RV + 1]
    delta = alpha0 - table[:, OWN : OWN + 1]

    def pick(weights):
        w = jnp.zeros((count, sblk), f32)
        for k, v in weights:
            w = jnp.where(lanes == k, v, w)
        return total(w * table)

    norm1 = pick(((NN, 1.0), (NV, -2.0 * delta), (VV, delta * delta)))
    product1 = pick(((NV, 1.0), (VV, -delta), (NW, -alpha0), (VW, alpha0 * delta)))
    ratio = norm1 / norm0
    alpha1 = norm1 / (product1 - ratio * norm1 / alpha0)
    coef[0:1, :] = jnp.broadcast_to(alpha0 + alpha1 * (1.0 + ratio), (1, nz))
    coef[1:2, :] = jnp.broadcast_to(-alpha1 * alpha0, (1, nz))


def out_kernel(r0, v1, coef, npr, inc, new_press, buf, rows, sems):
    comp, cx, cy, nz = buf.shape
    bpd = rows.shape[0]
    cr, cv = coef[0:1, :], coef[1:2, :]
    copies = []
    for c in range(comp):
        for x in range(cx):
            buf[c, x] = cr * r0[c, x] + cv * v1[c, x]
        copies.append(pltpu.make_async_copy(buf.at[c], inc.at[0, c], sems.at[c]))
        copies[-1].start()
    for l in range(bpd):
        rows[l : l + 1, :] = npr[0, l] - (cr * npr[1, l] + cv * npr[2, l])
    copies.append(pltpu.make_async_copy(rows, new_press, sems.at[comp]))
    copies[-1].start()
    for copy in copies:
        copy.wait()


def on_device(disp, force, kappa, sigma, gap0, pressure, mortar, partner, active):
    nb, ngx, ngy = (lax.axis_size(a) for a in ("body", "gx", "gy"))
    _, comp, cx, cy, nz = disp.shape
    bpd, sblk, _ = mortar.shape
    f32 = jnp.float32
    any_spec = pl.BlockSpec(memory_space=pl.ANY)
    vmem = pl.BlockSpec(memory_space=pltpu.VMEM)
    rows = cy + 2 * YB
    rowblk = ngx * bpd
    count = nb * ngx * ngy
    dma = pltpu.SemaphoreType.DMA
    full = pltpu.VMEM((bpd, sblk, nz), f32)
    most = max((comp + 1) * cx * cy, (comp + 1 + 2 * (comp - 1)) * 2 * (cy + cx + 2), count, bpd * sblk,
               3 * bpd * 4 * ngx)
    field = (comp, cx + 2, rows, nz)
    r0, v1, coef, npr = pl.pallas_call(
        functools.partial(kernel, nb, ngx, ngy),
        out_shape=(pltpu.VMEM((comp, cx, cy, nz), f32), pltpu.VMEM((comp, cx, cy, nz), f32), pltpu.VMEM((8, nz), f32),
                   pltpu.VMEM((3, bpd, 1, sblk), f32)),
        in_specs=[any_spec] * 9,
        out_specs=(vmem,) * 4,
        scratch_shapes=[
            pltpu.VMEM((bpd, sblk), f32),
            pltpu.VMEM((bpd, sblk), f32),
            pltpu.SMEM((bpd,), jnp.int32),
            pltpu.SMEM((bpd,), jnp.int32),
            pltpu.VMEM((comp + 1, cx + 2, rows, nz), f32),
            pltpu.VMEM(field, f32),
            pltpu.VMEM(field, f32),
            pltpu.VMEM((3, bpd, 1, sblk), f32),
            pltpu.VMEM((cx, cy, nz), f32),
            pltpu.VMEM((comp, cx, cy, nz), f32),
            pltpu.VMEM((cx, cy, nz), f32),
            pltpu.VMEM((bpd, sblk, sblk), f32),
            pltpu.VMEM((3, ngx, bpd, 1, sblk), f32),
            pltpu.VMEM((3, ngx, 3, bpd, 1, sblk), f32),
            pltpu.VMEM((3, rowblk + 2, 1, sblk), f32),
            full, full, full, full, full, full, full, full,
            pltpu.VMEM((8, 8, nz), f32),
            pltpu.VMEM((cy, nz), f32),
            pltpu.VMEM((count, 1, sblk), f32),
            pltpu.VMEM((most, 1, nz), f32),
            dma((7,)), dma((5,)), dma((3,)), dma((3,)), dma((1,)), dma((2,)), dma((2, 2)), dma((1,)), dma((2,)),
            dma((2,)),
        ],
        compiler_params=pltpu.CompilerParams(collective_id=0, has_side_effects=True,
                                             vmem_limit_bytes=60 * 1024 * 1024),
        name="newton_step",
    )(disp, force, kappa, sigma, gap0, pressure, mortar, partner, active)
    return pl.pallas_call(
        out_kernel,
        out_shape=(jax.ShapeDtypeStruct(disp.shape, f32), jax.ShapeDtypeStruct(gap0.shape, f32)),
        in_specs=[vmem] * 4,
        out_specs=(any_spec, any_spec),
        scratch_shapes=[pltpu.VMEM((comp, cx, cy, nz), f32), pltpu.VMEM((bpd, sblk), f32), dma((comp + 1,))],
        compiler_params=pltpu.CompilerParams(vmem_limit_bytes=4 * 1024 * 1024),
        name="newton_out",
    )(r0, v1, coef, npr)


def solution(mesh):
    placed = (
        P("body", None, "gx", "gy", None),
        P("body", None, "gx", "gy", None),
        P("body", "gx", "gy", None),
        P("body", "gx", "gy", None),
        P(("gx", "gy"), None),
        P(("gx", "gy"), None),
        P(("gx", "gy"), None, None),
        P(("gx", "gy")),
        P(("gx", "gy")),
    )
    return jax.shard_map(
        on_device,
        mesh=mesh,
        in_specs=placed,
        out_specs=(P("body", None, "gx", "gy", None), P(("gx", "gy"), None)),
        check_vma=False,
    )
```

```python
import functools

import jax
import jax.numpy as jnp
from jax import lax
from jax.experimental import pallas as pl
from jax.experimental.pallas import tpu as pltpu
from jax.sharding import PartitionSpec as P

MESH = pl.DeviceIdType.MESH
YB = 8
CORNERS = tuple((dx, dy) for dx in (-1, 1) for dy in (-1, 1))
DIRS = CORNERS + ((0, -1), (0, 1), (-1, 0), (1, 0))
RR, RV, VV, NN, NV, NW, VW, OWN = range(8)


def kernel(nb, ngx, ngy, disp, force, kappa, sigma, gap0_in, press_in, mortar, partner_in, active_in,
           r0_out, v1_out, coef, npr_out,
           gap0, press, partner, active, f0, f1, f2, npr, diag, force_v, sigma_v, mort, s1b, pbuf, ub, base, prs_f, t_f, ex_f, sl_f,
           st_f, gr_f, gv_f, acc, own_ref, final, dummy,
           ls, hr, hs, sr, ss, pr, pq, pn, ps, nps, fin):
    comp, cx, cy, nz = force_v.shape
    bpd, sblk = gap0.shape
    per = sblk // cy
    rowblk = ngx * bpd
    last = comp - 1
    b = lax.axis_index("body")
    gx = lax.axis_index("gx")
    gy = lax.axis_index("gy")
    count = nb * ngx * ngy
    me = (b * ngx + gx) * ngy + gy
    f32 = jnp.float32

    def far(at, k, size):
        if size & (size - 1):
            return lax.rem(at + k, size)
        for bit in (1 << i for i in range(size.bit_length() - 1)):
            if k & bit:
                at = at + bit - 2 * bit * lax.rem(at // bit, 2)
        return at

    def place_of(other):
        return {"body": other // (ngx * ngy), "gx": lax.rem(other // ngy, ngx), "gy": lax.rem(other, ngy)}

    def each_peer(act):
        if count <= 64:
            for k in range(1, count):
                act(k)
        else:
            pl.loop(1, count)(act)

    def exists(dx, dy):
        good = jnp.bool_(True)
        if dx < 0:
            good = good & (gx >= 1)
        if dx > 0:
            good = good & (gx < ngx - 1)
        if dy < 0:
            good = good & (gy >= 1)
        if dy > 0:
            good = good & (gy < ngy - 1)
        return good

    def as_int(flag):
        return flag.astype(jnp.int32)

    nys = as_int(exists(0, -1)) + as_int(exists(0, 1))
    nxs = as_int(exists(-1, 0)) + as_int(exists(1, 0))

    def sides(size):
        return (0,) if size == 1 else (1,) if size == 2 else (1, 2)

    def wait_rows(sem, rows):
        part = dummy.at[pl.ds(0, rows)]
        pltpu.make_async_copy(part, part, sem).wait()

    def wait_halo(sem, comps):
        for a in sides(ngx):
            for c in sides(ngy):
                rows = comps * (a * cy + c * cx + a * c)
                if rows:
                    pl.when((nxs == a) & (nys == c))(lambda: wait_rows(sem, rows))

    barrier = pltpu.get_barrier_semaphore()
    if ngy <= 4:
        expect = jnp.where(b == 1, ngx, 0)
        for dx, dy in DIRS:
            here = exists(dx, dy)
            expect = expect + as_int(here)

            @pl.when(here)
            def _():
                pl.semaphore_signal(barrier, inc=1, device_id={"gx": gx + dx, "gy": gy + dy}, device_id_type=MESH)
        for g in range(ngx):
            @pl.when(b == 0)
            def _():
                pl.semaphore_signal(barrier, inc=1, device_id={"body": 1, "gx": g}, device_id_type=MESH)
    else:
        each_peer(lambda k: pl.semaphore_signal(barrier, inc=1, device_id=place_of(lax.rem(me + k, count)),
                                                device_id_type=MESH))
        expect = count - 1

    inner = (pl.ds(1, cx), pl.ds(YB, cy))
    pltpu.make_async_copy(disp.at[0, last], f0.at[(last,) + inner], ls.at[0]).start()
    pltpu.make_async_copy(disp.at[0, pl.ds(0, last)], f0.at[(pl.ds(0, last),) + inner], ls.at[1]).start()
    pltpu.make_async_copy(kappa.at[0], f0.at[(comp,) + inner], ls.at[1]).start()
    pltpu.make_async_copy(gap0_in, gap0, ls.at[3]).start()
    pltpu.make_async_copy(press_in, press, ls.at[3]).start()
    pltpu.make_async_copy(partner_in, partner, ls.at[4]).start()
    pltpu.make_async_copy(active_in, active, ls.at[5]).start()
    pltpu.make_async_copy(mortar, mort, ls.at[6]).start()
    pltpu.make_async_copy(sigma.at[0], sigma_v, ls.at[2]).start()
    pltpu.make_async_copy(force.at[0], force_v, ls.at[2]).start()

    for side, x in ((-1, 0), (1, cx + 1)):
        @pl.when(jnp.logical_not(exists(side, 0)))
        def _():
            for f in (f0, f1, f2):
                for c in range(f.shape[0]):
                    f[c, x, YB - 1 : YB] = jnp.zeros((1, nz), f32)
                    f[c, x, YB : YB + cy] = jnp.zeros((cy, nz), f32)
                    f[c, x, YB + cy : YB + cy + 1] = jnp.zeros((1, nz), f32)
    for side, y in ((-1, YB - 1), (1, YB + cy)):
        @pl.when(jnp.logical_not(exists(0, side)))
        def _():
            for f in (f0, f1, f2):
                for c in range(f.shape[0]):
                    for x in range(cx + 2):
                        f[c, x, y : y + 1] = jnp.zeros((1, nz), f32)
            for g in range(ngx):
                for k in range(3):
                    for l in range(bpd):
                        pbuf[1 + side, g, k, l] = jnp.zeros((1, sblk), f32)
    for d in range(3):
        for q in (0, rowblk + 1):
            ub[d, q] = jnp.zeros((1, sblk), f32)
    for k in range(8):
        acc[k] = jnp.zeros((8, nz), f32)

    lane = lax.broadcasted_iota(jnp.int32, (sblk, nz), 1)
    eye = lax.broadcasted_iota(jnp.int32, (sblk, nz), 0) == lane
    first_lane = lane == 0
    lane_row = lax.broadcasted_iota(jnp.int32, (cy, nz), 1)
    left_w = jnp.where(lane_row == 0, 0.0, 0.5)
    right_w = jnp.where(lane_row == nz - 1, 0.0, 0.5)
    lane_one = lax.broadcasted_iota(jnp.int32, (1, nz), 1)
    block_of = lax.broadcasted_iota(jnp.int32, (rowblk, sblk), 0)
    block_f = block_of.astype(f32)

    def to_full(row):
        return jnp.broadcast_to(jnp.sum(jnp.where(eye, row, 0.0), axis=1, keepdims=True), (sblk, nz))

    def to_row(full):
        return jnp.sum(jnp.where(eye, full, 0.0), axis=0, keepdims=True)

    def tz(v):
        return v + left_w * pltpu.roll(v, 1, 1) + right_w * pltpu.roll(v, nz - 1, 1)

    def block(f, l):
        return f[last, 1 + l * per : 1 + (l + 1) * per, YB : YB + cy, :].reshape(sblk, nz)

    def first_of(f, l):
        return jnp.broadcast_to(block(f, l)[:, 0:1], (sblk, nz))

    def take_off(f, l, full):
        xs = slice(1 + l * per, 1 + (l + 1) * per)
        f[last, xs, YB : YB + cy, :] = (block(f, l) - jnp.where(first_lane, full, 0.0)).reshape(per, cy, nz)

    def part(delta, size, base_at, src_base):
        if delta == 0:
            return pl.ds(src_base, size), pl.ds(base_at, size)
        if delta < 0:
            return pl.ds(src_base, 1), pl.ds(base_at + size, 1)
        return pl.ds(src_base + size - 1, 1), pl.ds(base_at - 1, 1)

    def halo_send(f, at, size, send_sem, recv_sem):
        cs = pl.ds(at, size)
        for dx, dy in DIRS:
            @pl.when(exists(dx, dy))
            def _():
                sx, tx = part(dx, cx, 1, 1)
                sy, ty = part(dy, cy, YB, YB)
                pltpu.make_async_remote_copy(
                    src_ref=f.at[cs, sx, sy], dst_ref=f.at[cs, tx, ty], send_sem=send_sem, recv_sem=recv_sem,
                    device_id={"gx": gx + dx, "gy": gy + dy}, device_id_type=MESH).start()

    def halo_send_args():
        for dx, dy in DIRS:
            @pl.when(exists(dx, dy))
            def _():
                sx, tx = part(dx, cx, 1, 0)
                sy, ty = part(dy, cy, YB, 0)
                for src, dst in ((disp.at[0, :, sx, sy], f0.at[pl.ds(0, comp), tx, ty]),
                                 (kappa.at[:, sx, sy], f0.at[pl.ds(comp, 1), tx, ty])):
                    pltpu.make_async_remote_copy(
                        src_ref=src, dst_ref=dst, send_sem=hs.at[0], recv_sem=hr.at[0],
                        device_id={"gx": gx + dx, "gy": gy + dy}, device_id_type=MESH).start()

    def surf_send(r):
        for k in reversed(range(ngx)):
            pltpu.make_async_remote_copy(
                src_ref=s1b.at[r, gx], dst_ref=s1b.at[r, gx], send_sem=ss.at[0], recv_sem=sr.at[r],
                device_id={"body": 0, "gx": far(gx, k, ngx)}, device_id_type=MESH).start()

    def surface_rows(f, r):
        for l in range(bpd):
            s1b[r, gx, l] = to_row(first_of(f, l))

    def pulled_send(first, size, r):
        ks = pl.ds(first, size)

        def go(bo, g, sem):
            pltpu.make_async_remote_copy(
                src_ref=pbuf.at[1, gx, ks], dst_ref=pbuf.at[1, gx, ks], send_sem=ps.at[0], recv_sem=sem,
                device_id={"body": bo, "gx": g}, device_id_type=MESH).start()
        go(1, gx, pq.at[r])
        for k in reversed(range(1, ngx)):
            go(1, far(gx, k, ngx), pr.at[r])
            go(0, far(gx, k, ngx), pr.at[r])

    def pass_on(r, first, size):
        ks = pl.ds(first, size)
        wait_rows(pq.at[r], size * bpd)
        for s in (-1, 1):
            @pl.when(exists(0, s))
            def _():
                for k in reversed(range(ngx)):
                    pltpu.make_async_remote_copy(
                        src_ref=pbuf.at[1, gx, ks], dst_ref=pbuf.at[1 - s, gx, ks], send_sem=ps.at[0],
                        recv_sem=pn.at[r, (1 - s) // 2], device_id={"gx": far(gx, k, ngx), "gy": gy + s},
                        device_id_type=MESH).start()

    def expand(d, k):
        u = jnp.zeros((rowblk, sblk), f32)
        for g in range(ngx):
            for l in range(bpd):
                u = u + jnp.where(block_f == pbuf[d, g, 1, l], pbuf[d, g, k, l], 0.0)
        return u

    def ring_fix(f, r, k, size):
        if ngx > 1:
            wait_rows(pr.at[r], (ngx - 1) * size * bpd)
        ub[1, 1 : 1 + rowblk] = expand(1, k).reshape(rowblk, 1, sblk)

        def row(d, j):
            return ub[d, gx * bpd + j]

        for l in range(bpd):
            take_off(f, l, to_full(row(1, 1 + l)))
        for j, x, at in ((0, 0, sblk - cy), (bpd + 1, cx + 1, 0)):
            col = jnp.sum(jnp.where(eye[at : at + cy], row(1, j), 0.0), axis=1, keepdims=True)
            f[last, x, YB : YB + cy, :] = f[last, x, YB : YB + cy, :] - jnp.where(lane_row == 0, col, 0.0)
        if r == 0:
            pass_on(1, 2, 1)
        for d, y, off in ((0, YB - 1, cy - 1), (2, YB + cy, 0)):
            pl.when(exists(0, d - 1))(lambda: wait_rows(pn.at[r, d // 2], ngx * size * bpd))
            ub[d, 1 : 1 + rowblk] = expand(d, k).reshape(rowblk, 1, sblk)
            for xi in range(cx + 2):
                j = (xi - 1 + per) // per
                at = ((xi - 1 + per) % per) * cy + off
                val = pltpu.roll(row(d, j), (nz - at) % nz, 1)
                f[last, xi, y : y + 1, :] = f[last, xi, y : y + 1, :] - jnp.where(lane_one == 0, val, 0.0)

    def apply(f, c, emit):
        window = []
        for x in range(cx + 2):
            kap = [f0[comp, x, YB + s : YB + s + cy, :] for s in (-1, 0, 1)]
            val = [f[c, x, YB + s : YB + s + cy, :] for s in (-1, 0, 1)]
            window.append((val[1] + 0.5 * (val[0] + val[2]),
                           kap[1] * val[1] + 0.5 * (kap[0] * val[0] + kap[2] * val[2])))
            if x >= 2:
                p = window[x - 1][0] + 0.5 * (window[x - 2][0] + window[x][0])
                q = window[x - 1][1] + 0.5 * (window[x - 2][1] + window[x][1])
                k0 = f0[comp, x - 1, YB : YB + cy, :]
                v0 = f[c, x - 1, YB : YB + cy, :]
                emit(c, x - 2, diag[x - 2] * v0 - k0 * tz(p) - tz(q))

    def make_diag():
        window = []
        for x in range(cx + 2):
            kap = [f0[comp, x, YB + s : YB + s + cy, :] for s in (-1, 0, 1)]
            window.append(kap[1] + 0.5 * (kap[0] + kap[2]))
            if x >= 2:
                p = window[x - 1] + 0.5 * (window[x - 2] + window[x])
                diag[x - 2] = sigma_v[x - 2] + 8.0 * f0[comp, x - 1, YB : YB + cy, :] + tz(p)

    def emit_rhs(c, x, val):
        f1[c, 1 + x, YB : YB + cy, :] = force_v[c, x] - val

    def emit_v1(c, x, val):
        f2[c, 1 + x, YB : YB + cy, :] = val

    def r0_of(c, x):
        return f1[c, 1 + x, YB : YB + cy, :]

    def v1_of(c, x):
        return f2[c, 1 + x, YB : YB + cy, :]

    def fold(v):
        return jnp.sum(v.reshape(cy // 8, 8, nz), axis=0)

    def gather(c, wanted, fields):
        sums = {}
        for x in range(cx):
            for k, (left, right) in wanted.items():
                term = fold(fields(x)[left] * fields(x)[right])
                sums[k] = sums[k] + term if k in sums else term
        for k, v in sums.items():
            acc[k] = acc[k] + v

    def dots(c):
        gather(c, {RR: (0, 0), RV: (0, 1), VV: (1, 1)}, lambda x: (r0_of(c, x), v1_of(c, x)))

    def total(v):
        return jnp.sum(jnp.sum(v, axis=0, keepdims=True), axis=1, keepdims=True)

    def choose_own():
        rv, vv = total(acc[RV]), total(acc[VV])
        own = jnp.where(vv > 0.0, rv / jnp.where(vv > 0.0, vv, 1.0), 0.0)
        own_ref[...] = jnp.broadcast_to(own, (cy, nz))

    def near_dots(c):
        own = own_ref[...]
        gather(c, {NN: (0, 0), NV: (0, 1)}, lambda x: (r0_of(c, x) - own * v1_of(c, x), v1_of(c, x)))

    def image_dots(c, more):
        own = own_ref[...]
        sums = {}

        def emit(c, x, val):
            v = v1_of(c, x)
            r = r0_of(c, x)
            near = r - own * v
            terms = {NW: near * val, VW: v * val}
            if more:
                terms.update({RV: r * v, VV: v * v, NN: near * near, NV: near * v})
            for k, t in terms.items():
                sums[k] = sums[k] + fold(t) if k in sums else fold(t)
        apply(f2, c, emit)
        for k, v in sums.items():
            acc[k] = acc[k] + v

    def first_comps(act):
        @pl.loop(0, last)
        def _(c):
            act(c)

    def gap_of(l, s1):
        picked = jnp.sum(jnp.where(block_of == partner[l], s1, 0.0), axis=0, keepdims=True)
        return base[l] - jnp.broadcast_to(jnp.sum(mort[l] * picked, axis=1, keepdims=True), (sblk, nz))

    def pull(l, k, t):
        pbuf[1, gx, k, l] = jnp.sum(mort[l] * t, axis=0, keepdims=True)

    def surf_rows(r):
        return s1b[r].reshape(rowblk, sblk)

    def send_final():
        sub = lax.broadcasted_iota(jnp.int32, (8, nz), 0)
        stack = jnp.zeros((8, nz), f32)
        for k in range(OWN):
            stack = jnp.where(sub == k, jnp.broadcast_to(jnp.sum(acc[k], axis=0, keepdims=True), (8, nz)), stack)
        lanes = lax.broadcasted_iota(jnp.int32, (8, nz), 1)
        stack = jnp.where((sub == OWN) & (lanes == 0), own_ref[0:8, :], stack)
        final[me] = jnp.sum(jnp.where(sub == lanes, jnp.sum(stack, axis=1, keepdims=True), 0.0), axis=0, keepdims=True)

        def go(place):
            pltpu.make_async_remote_copy(
                src_ref=final.at[me], dst_ref=final.at[me], send_sem=fin.at[0], recv_sem=fin.at[1],
                device_id=place, device_id_type=MESH).start()
        if count <= 64:
            for kx in reversed(range(ngx)):
                for ky in reversed(range(ngy)):
                    for kb in reversed(range(nb)):
                        if kx or ky or kb:
                            go({"body": far(b, kb, nb), "gx": far(gx, kx, ngx), "gy": far(gy, ky, ngy)})
        else:
            each_peer(lambda k: go(place_of(lax.rem(me + k, count))))

    pl.semaphore_wait(barrier, expect)

    @pl.when(b == 1)
    def _():
        wait_rows(ls.at[0], cx * cy)
        surface_rows(f0, 0)
        surf_send(0)

    halo_send_args()

    @pl.when(b == 1)
    def _():
        wait_rows(ls.at[1], comp * cx * cy)
        wait_rows(ls.at[2], (comp + 1) * cx * cy)
        wait_halo(hr.at[0], comp + 1)
        make_diag()
        apply(f0, last, emit_rhs)
        surface_rows(f1, 1)
        surf_send(1)
        halo_send(f1, last, 1, hs.at[1], hr.at[2])
        pass_on(0, 0, 2)
        first_comps(lambda c: apply(f0, c, emit_rhs))
        halo_send(f1, 0, last, hs.at[0], hr.at[1])

        wait_halo(hr.at[1], last)
        first_comps(lambda c: apply(f1, c, emit_v1))
        halo_send(f2, 0, last, hs.at[0], hr.at[3])
        first_comps(dots)
        choose_own()
        first_comps(near_dots)
        wait_halo(hs.at[1], 1)
        wait_halo(hr.at[2], 1)
        ring_fix(f1, 0, 0, 2)
        apply(f1, last, emit_v1)
        surface_rows(f2, 2)
        surf_send(2)
        halo_send(f2, last, 1, hs.at[2], hr.at[4])
        gather(last, {RR: (0, 0)}, lambda x: (r0_of(last, x),))

        wait_halo(hr.at[3], last)
        first_comps(lambda c: image_dots(c, False))
        wait_halo(hs.at[2], 1)
        wait_halo(hr.at[4], 1)
        ring_fix(f2, 1, 2, 1)
        image_dots(last, True)
        send_final()

    @pl.when(b == 0)
    def _():
        for k in range(4):
            sem, rows = ((ls.at[0], cx * cy), (ls.at[3], 2 * bpd), (ls.at[6], bpd * sblk), (ls.at[1], comp * cx * cy))[k]
            wait_rows(sem, rows)
        pltpu.make_async_copy(partner_in, partner, ls.at[4]).wait()
        pltpu.make_async_copy(active_in, active, ls.at[5]).wait()
        for l in range(bpd):
            base[l] = to_full(gap0[l : l + 1, :]) - first_of(f0, l)
            prs_f[l] = to_full(press[l : l + 1, :])
            pbuf[1, gx, 1, l] = jnp.full((1, sblk), partner[l].astype(f32))
        wait_rows(sr.at[0], ngx * bpd)
        s1 = surf_rows(0)
        for l in range(bpd):
            gap = gap_of(l, s1)
            prs = prs_f[l]
            radius = jnp.sqrt(gap * gap + prs * prs + 0.01)
            per_radius = 1.0 / radius
            per_divisor = 1.0 / ((1.0 - prs * per_radius) + 0.5)
            flag = active[l].astype(f32)
            excess = (gap + prs - radius) * per_divisor
            slope = (1.0 - gap * per_radius) * per_divisor
            t = flag * (prs - excess)
            pull(l, 0, t)
            t_f[l] = t
            ex_f[l] = excess
            sl_f[l] = slope
            st_f[l] = flag * slope
        pulled_send(0, 2, 0)
        wait_rows(ls.at[2], (comp + 1) * cx * cy)
        wait_halo(hr.at[0], comp + 1)
        make_diag()
        first_comps(lambda c: apply(f0, c, emit_rhs))
        halo_send(f1, 0, last, hs.at[0], hr.at[1])
        apply(f0, last, emit_rhs)
        for l in range(bpd):
            take_off(f1, l, t_f[l])
        halo_send(f1, last, 1, hs.at[1], hr.at[2])
        for l in range(bpd):
            base[l] = -first_of(f1, l)

        wait_rows(sr.at[1], ngx * bpd)
        if ngx > 1:
            wait_rows(pr.at[0], (ngx - 1) * 2 * bpd)
        s1 = surf_rows(1) - expand(1, 0)
        for l in range(bpd):
            gap = gap_of(l, s1)
            t = st_f[l] * gap
            pull(l, 2, t)
            t_f[l] = t
            gr_f[l] = gap
        pulled_send(2, 1, 1)
        wait_halo(hr.at[1], last)
        first_comps(lambda c: apply(f1, c, emit_v1))
        halo_send(f2, 0, last, hs.at[0], hr.at[3])
        wait_halo(hr.at[2], 1)
        apply(f1, last, emit_v1)
        for l in range(bpd):
            take_off(f2, l, t_f[l])
        halo_send(f2, last, 1, hs.at[2], hr.at[4])
        for l in range(bpd):
            base[l] = -first_of(f2, l)
        first_comps(dots)
        choose_own()
        dots(last)
        pl.loop(0, comp)(near_dots)
        wait_halo(hr.at[3], last)
        wait_halo(hr.at[4], 1)
        pl.loop(0, comp)(lambda c: image_dots(c, False))

        wait_rows(sr.at[2], ngx * bpd)
        if ngx > 1:
            wait_rows(pr.at[1], (ngx - 1) * bpd)
        s1 = surf_rows(2) - expand(1, 2)
        own = own_ref[0:1, :]
        for l in range(bpd):
            gap = gap_of(l, s1)
            gv_f[l] = gap
            weighted = st_f[l] * gap
            for k, left in ((NW, gr_f[l] - own * gap), (VW, gap)):
                row = jnp.sum(weighted * left, axis=0, keepdims=True)
                acc[k, 0:1] = acc[k, 0:1] + jnp.where(lane_one == 0, row, 0.0)
        send_final()
        for l in range(bpd):
            flag = active[l].astype(f32)
            npr[0, l] = flag * (press[l : l + 1, :] - to_row(ex_f[l]))
            npr[1, l] = flag * to_row(sl_f[l] * gr_f[l])
            npr[2, l] = flag * to_row(sl_f[l] * gv_f[l])
        pltpu.make_async_remote_copy(src_ref=npr, dst_ref=npr, send_sem=nps.at[0], recv_sem=nps.at[1],
                                     device_id={"body": 1}, device_id_type=MESH).start()

    @pl.when(b == 1)
    def _():
        wait_rows(ls.at[3], 2 * bpd)
        wait_rows(ls.at[6], bpd * sblk)
        pltpu.make_async_copy(partner_in, partner, ls.at[4]).wait()
        pltpu.make_async_copy(active_in, active, ls.at[5]).wait()
        wait_rows(ss.at[0], 3 * ngx * bpd)
        for c in sides(ngy):
            if c:
                pl.when(nys == c)(lambda: wait_rows(ps.at[0], 3 * bpd * c * ngx))
        wait_rows(nps.at[1], 3 * bpd)

    @pl.when(b == 0)
    def _():
        wait_rows(ps.at[0], 3 * bpd * (2 * ngx - 1))
        wait_halo(hs.at[1], 1)
        wait_halo(hs.at[2], 1)
        wait_rows(nps.at[0], 3 * bpd)

    wait_halo(hs.at[0], comp + 1 + 2 * last)
    wait_rows(fin.at[0], count - 1)
    for c in range(comp):
        for x in range(cx):
            r0_out[c, x] = r0_of(c, x)
            v1_out[c, x] = v1_of(c, x)
    npr_out[...] = npr[...]

    wait_rows(fin.at[1], count - 1)
    table = final[...].reshape(count, sblk)
    lanes = lax.broadcasted_iota(jnp.int32, (count, sblk), 1)
    sums = jnp.sum(table, axis=0, keepdims=True)
    norm0 = sums[:, RR : RR + 1]
    alpha0 = norm0 / sums[:, RV : RV + 1]
    delta = alpha0 - table[:, OWN : OWN + 1]

    def pick(weights):
        w = jnp.zeros((count, sblk), f32)
        for k, v in weights:
            w = jnp.where(lanes == k, v, w)
        return total(w * table)

    norm1 = pick(((NN, 1.0), (NV, -2.0 * delta), (VV, delta * delta)))
    product1 = pick(((NV, 1.0), (VV, -delta), (NW, -alpha0), (VW, alpha0 * delta)))
    ratio = norm1 / norm0
    alpha1 = norm1 / (product1 - ratio * norm1 / alpha0)
    coef[0:1, :] = jnp.broadcast_to(alpha0 + alpha1 * (1.0 + ratio), (1, nz))
    coef[1:2, :] = jnp.broadcast_to(-alpha1 * alpha0, (1, nz))


def out_kernel(r0, v1, coef, npr, inc, new_press, buf, rows, sems):
    comp, cx, cy, nz = buf.shape
    bpd = rows.shape[0]
    cr, cv = coef[0:1, :], coef[1:2, :]
    copies = []
    for c in range(comp):
        for x in range(cx):
            buf[c, x] = cr * r0[c, x] + cv * v1[c, x]
        copies.append(pltpu.make_async_copy(buf.at[c], inc.at[0, c], sems.at[c]))
        copies[-1].start()
    for l in range(bpd):
        rows[l : l + 1, :] = npr[0, l] - (cr * npr[1, l] + cv * npr[2, l])
    copies.append(pltpu.make_async_copy(rows, new_press, sems.at[comp]))
    copies[-1].start()
    for copy in copies:
        copy.wait()


def on_device(disp, force, kappa, sigma, gap0, pressure, mortar, partner, active):
    nb, ngx, ngy = (lax.axis_size(a) for a in ("body", "gx", "gy"))
    _, comp, cx, cy, nz = disp.shape
    bpd, sblk, _ = mortar.shape
    f32 = jnp.float32
    any_spec = pl.BlockSpec(memory_space=pl.ANY)
    vmem = pl.BlockSpec(memory_space=pltpu.VMEM)
    rows = cy + 2 * YB
    rowblk = ngx * bpd
    count = nb * ngx * ngy
    dma = pltpu.SemaphoreType.DMA
    full = pltpu.VMEM((bpd, sblk, nz), f32)
    most = max((comp + 1) * cx * cy, (comp + 1 + 2 * (comp - 1)) * 2 * (cy + cx + 2), count, bpd * sblk,
               3 * bpd * 4 * ngx)
    field = (comp, cx + 2, rows, nz)
    r0, v1, coef, npr = pl.pallas_call(
        functools.partial(kernel, nb, ngx, ngy),
        out_shape=(pltpu.VMEM((comp, cx, cy, nz), f32), pltpu.VMEM((comp, cx, cy, nz), f32), pltpu.VMEM((8, nz), f32),
                   pltpu.VMEM((3, bpd, 1, sblk), f32)),
        in_specs=[any_spec] * 9,
        out_specs=(vmem,) * 4,
        scratch_shapes=[
            pltpu.VMEM((bpd, sblk), f32),
            pltpu.VMEM((bpd, sblk), f32),
            pltpu.SMEM((bpd,), jnp.int32),
            pltpu.SMEM((bpd,), jnp.int32),
            pltpu.VMEM((comp + 1, cx + 2, rows, nz), f32),
            pltpu.VMEM(field, f32),
            pltpu.VMEM(field, f32),
            pltpu.VMEM((3, bpd, 1, sblk), f32),
            pltpu.VMEM((cx, cy, nz), f32),
            pltpu.VMEM((comp, cx, cy, nz), f32),
            pltpu.VMEM((cx, cy, nz), f32),
            pltpu.VMEM((bpd, sblk, sblk), f32),
            pltpu.VMEM((3, ngx, bpd, 1, sblk), f32),
            pltpu.VMEM((3, ngx, 3, bpd, 1, sblk), f32),
            pltpu.VMEM((3, rowblk + 2, 1, sblk), f32),
            full, full, full, full, full, full, full, full,
            pltpu.VMEM((8, 8, nz), f32),
            pltpu.VMEM((cy, nz), f32),
            pltpu.VMEM((count, 1, sblk), f32),
            pltpu.VMEM((most, 1, nz), f32),
            dma((7,)), dma((5,)), dma((3,)), dma((3,)), dma((1,)), dma((2,)), dma((2,)), dma((2, 2)), dma((1,)), dma((2,)),
            dma((2,)),
        ],
        compiler_params=pltpu.CompilerParams(collective_id=0, has_side_effects=True,
                                             vmem_limit_bytes=60 * 1024 * 1024),
        name="newton_step",
    )(disp, force, kappa, sigma, gap0, pressure, mortar, partner, active)
    return pl.pallas_call(
        out_kernel,
        out_shape=(jax.ShapeDtypeStruct(disp.shape, f32), jax.ShapeDtypeStruct(gap0.shape, f32)),
        in_specs=[vmem] * 4,
        out_specs=(any_spec, any_spec),
        scratch_shapes=[pltpu.VMEM((comp, cx, cy, nz), f32), pltpu.VMEM((bpd, sblk), f32), dma((comp + 1,))],
        compiler_params=pltpu.CompilerParams(vmem_limit_bytes=4 * 1024 * 1024),
        name="newton_out",
    )(r0, v1, coef, npr)


def solution(mesh):
    placed = (
        P("body", None, "gx", "gy", None),
        P("body", None, "gx", "gy", None),
        P("body", "gx", "gy", None),
        P("body", "gx", "gy", None),
        P(("gx", "gy"), None),
        P(("gx", "gy"), None),
        P(("gx", "gy"), None, None),
        P(("gx", "gy")),
        P(("gx", "gy")),
    )
    return jax.shard_map(
        on_device,
        mesh=mesh,
        in_specs=placed,
        out_specs=(P("body", None, "gx", "gy", None), P(("gx", "gy"), None)),
        check_vma=False,
    )
```

```python
import functools

import jax
import jax.numpy as jnp
from jax import lax
from jax.experimental import pallas as pl
from jax.experimental.pallas import tpu as pltpu
from jax.sharding import PartitionSpec as P

MESH = pl.DeviceIdType.MESH
YB = 8
CORNERS = tuple((dx, dy) for dx in (-1, 1) for dy in (-1, 1))
ALONG_Y = ((0, -1), (0, 1))
ACROSS_X = CORNERS + ((-1, 0), (1, 0))
FACES_X = ((-1, 0), (1, 0))
DIRS = CORNERS + ALONG_Y + FACES_X
RR, RV, VV, NN, NV, NW, VW, OWN = range(8)


def kernel(nb, ngx, ngy, disp, force, kappa, sigma, gap0_in, press_in, mortar, partner_in, active_in,
           r0_out, v1_out, coef, npr_out,
           gap0, press, partner, active, f0, f1, f2, npr, diag, force_v, sigma_v, mort, s1b, pbuf, ub, base, prs_f, t_f, ex_f, sl_f,
           st_f, gr_f, gv_f, acc, own_ref, final, dummy,
           ls, hr, hs, sr, ss, pr, pq, pn, ps, nps, fin):
    comp, cx, cy, nz = force_v.shape
    bpd, sblk = gap0.shape
    per = sblk // cy
    rowblk = ngx * bpd
    last = comp - 1
    b = lax.axis_index("body")
    gx = lax.axis_index("gx")
    gy = lax.axis_index("gy")
    count = nb * ngx * ngy
    me = (b * ngx + gx) * ngy + gy
    f32 = jnp.float32

    def far(at, k, size):
        if size & (size - 1):
            return lax.rem(at + k, size)
        for bit in (1 << i for i in range(size.bit_length() - 1)):
            if k & bit:
                at = at + bit - 2 * bit * lax.rem(at // bit, 2)
        return at

    def place_of(other):
        return {"body": other // (ngx * ngy), "gx": lax.rem(other // ngy, ngx), "gy": lax.rem(other, ngy)}

    def each_peer(act):
        if count <= 64:
            for k in range(1, count):
                act(k)
        else:
            pl.loop(1, count)(act)

    def exists(dx, dy):
        good = jnp.bool_(True)
        if dx < 0:
            good = good & (gx >= 1)
        if dx > 0:
            good = good & (gx < ngx - 1)
        if dy < 0:
            good = good & (gy >= 1)
        if dy > 0:
            good = good & (gy < ngy - 1)
        return good

    def as_int(flag):
        return flag.astype(jnp.int32)

    nys = as_int(exists(0, -1)) + as_int(exists(0, 1))
    nxs = as_int(exists(-1, 0)) + as_int(exists(1, 0))

    def sides(size):
        return (0,) if size == 1 else (1,) if size == 2 else (1, 2)

    def wait_rows(sem, rows):
        part = dummy.at[pl.ds(0, rows)]
        pltpu.make_async_copy(part, part, sem).wait()

    def wait_halo(sem, comps):
        for a in sides(ngx):
            for c in sides(ngy):
                rows = comps * (a * cy + c * cx + a * c)
                if rows:
                    pl.when((nxs == a) & (nys == c))(lambda: wait_rows(sem, rows))

    barrier = pltpu.get_barrier_semaphore()
    if ngy <= 4:
        expect = jnp.where(b == 1, ngx, 0)
        for dx, dy in DIRS:
            here = exists(dx, dy)
            expect = expect + as_int(here)

            @pl.when(here)
            def _():
                pl.semaphore_signal(barrier, inc=1, device_id={"gx": gx + dx, "gy": gy + dy}, device_id_type=MESH)
        for g in range(ngx):
            @pl.when(b == 0)
            def _():
                pl.semaphore_signal(barrier, inc=1, device_id={"body": 1, "gx": g}, device_id_type=MESH)
    else:
        each_peer(lambda k: pl.semaphore_signal(barrier, inc=1, device_id=place_of(lax.rem(me + k, count)),
                                                device_id_type=MESH))
        expect = count - 1

    inner = (pl.ds(1, cx), pl.ds(YB, cy))
    pltpu.make_async_copy(disp.at[0, last], f0.at[(last,) + inner], ls.at[0]).start()
    pltpu.make_async_copy(disp.at[0, pl.ds(0, last)], f0.at[(pl.ds(0, last),) + inner], ls.at[1]).start()
    pltpu.make_async_copy(kappa.at[0], f0.at[(comp,) + inner], ls.at[1]).start()
    pltpu.make_async_copy(gap0_in, gap0, ls.at[3]).start()
    pltpu.make_async_copy(press_in, press, ls.at[3]).start()
    pltpu.make_async_copy(partner_in, partner, ls.at[4]).start()
    pltpu.make_async_copy(active_in, active, ls.at[5]).start()
    pltpu.make_async_copy(mortar, mort, ls.at[6]).start()
    pltpu.make_async_copy(sigma.at[0], sigma_v, ls.at[2]).start()
    pltpu.make_async_copy(force.at[0], force_v, ls.at[2]).start()

    for side, x in ((-1, 0), (1, cx + 1)):
        @pl.when(jnp.logical_not(exists(side, 0)))
        def _():
            for f in (f0, f1, f2):
                for c in range(f.shape[0]):
                    f[c, x, YB - 1 : YB] = jnp.zeros((1, nz), f32)
                    f[c, x, YB : YB + cy] = jnp.zeros((cy, nz), f32)
                    f[c, x, YB + cy : YB + cy + 1] = jnp.zeros((1, nz), f32)
    for side, y in ((-1, YB - 1), (1, YB + cy)):
        @pl.when(jnp.logical_not(exists(0, side)))
        def _():
            for f in (f0, f1, f2):
                for c in range(f.shape[0]):
                    for x in range(cx + 2):
                        f[c, x, y : y + 1] = jnp.zeros((1, nz), f32)
            for g in range(ngx):
                for k in range(3):
                    for l in range(bpd):
                        pbuf[1 + side, g, k, l] = jnp.zeros((1, sblk), f32)
    for d in range(3):
        for q in (0, rowblk + 1):
            ub[d, q] = jnp.zeros((1, sblk), f32)
    for k in range(8):
        acc[k] = jnp.zeros((8, nz), f32)

    lane = lax.broadcasted_iota(jnp.int32, (sblk, nz), 1)
    eye = lax.broadcasted_iota(jnp.int32, (sblk, nz), 0) == lane
    first_lane = lane == 0
    lane_row = lax.broadcasted_iota(jnp.int32, (cy, nz), 1)
    left_w = jnp.where(lane_row == 0, 0.0, 0.5)
    right_w = jnp.where(lane_row == nz - 1, 0.0, 0.5)
    lane_one = lax.broadcasted_iota(jnp.int32, (1, nz), 1)
    block_of = lax.broadcasted_iota(jnp.int32, (rowblk, sblk), 0)
    block_f = block_of.astype(f32)

    def to_full(row):
        return jnp.broadcast_to(jnp.sum(jnp.where(eye, row, 0.0), axis=1, keepdims=True), (sblk, nz))

    def to_row(full):
        return jnp.sum(jnp.where(eye, full, 0.0), axis=0, keepdims=True)

    def tz(v):
        return v + left_w * pltpu.roll(v, 1, 1) + right_w * pltpu.roll(v, nz - 1, 1)

    def block(f, l):
        return f[last, 1 + l * per : 1 + (l + 1) * per, YB : YB + cy, :].reshape(sblk, nz)

    def first_of(f, l):
        return jnp.broadcast_to(block(f, l)[:, 0:1], (sblk, nz))

    def take_off(f, l, full):
        xs = slice(1 + l * per, 1 + (l + 1) * per)
        f[last, xs, YB : YB + cy, :] = (block(f, l) - jnp.where(first_lane, full, 0.0)).reshape(per, cy, nz)

    def part(delta, size, base_at, src_base):
        if delta == 0:
            return pl.ds(src_base, size), pl.ds(base_at, size)
        if delta < 0:
            return pl.ds(src_base, 1), pl.ds(base_at + size, 1)
        return pl.ds(src_base + size - 1, 1), pl.ds(base_at - 1, 1)

    def halo_send(f, at, size, send_sem, recv_sem, dirs):
        cs = pl.ds(at, size)
        for dx, dy in dirs:
            @pl.when(exists(dx, dy))
            def _():
                sx, tx = part(dx, cx, 1, 1)
                sy, ty = part(dy, cy, YB, YB)
                pltpu.make_async_remote_copy(
                    src_ref=f.at[cs, sx, sy], dst_ref=f.at[cs, tx, ty], send_sem=send_sem, recv_sem=recv_sem,
                    device_id={"gx": gx + dx, "gy": gy + dy}, device_id_type=MESH).start()

    def halo_send_args(dirs):
        for dx, dy in dirs:
            @pl.when(exists(dx, dy))
            def _():
                sx, tx = part(dx, cx, 1, 0)
                sy, ty = part(dy, cy, YB, 0)
                for src, dst in ((disp.at[0, :, sx, sy], f0.at[pl.ds(0, comp), tx, ty]),
                                 (kappa.at[:, sx, sy], f0.at[pl.ds(comp, 1), tx, ty])):
                    pltpu.make_async_remote_copy(
                        src_ref=src, dst_ref=dst, send_sem=hs.at[0], recv_sem=hr.at[0],
                        device_id={"gx": gx + dx, "gy": gy + dy}, device_id_type=MESH).start()

    def surf_send(r):
        for k in reversed(range(ngx)):
            pltpu.make_async_remote_copy(
                src_ref=s1b.at[r, gx], dst_ref=s1b.at[r, gx], send_sem=ss.at[0], recv_sem=sr.at[r],
                device_id={"body": 0, "gx": far(gx, k, ngx)}, device_id_type=MESH).start()

    def surface_rows(f, r):
        for l in range(bpd):
            s1b[r, gx, l] = to_row(first_of(f, l))

    def pulled_send(first, size, r):
        ks = pl.ds(first, size)

        def go(bo, g, sem):
            pltpu.make_async_remote_copy(
                src_ref=pbuf.at[1, gx, ks], dst_ref=pbuf.at[1, gx, ks], send_sem=ps.at[0], recv_sem=sem,
                device_id={"body": bo, "gx": g}, device_id_type=MESH).start()
        go(1, gx, pq.at[r])
        for k in reversed(range(1, ngx)):
            go(1, far(gx, k, ngx), pr.at[r])
            go(0, far(gx, k, ngx), pr.at[r])

    def pass_on(r, first, size):
        ks = pl.ds(first, size)
        wait_rows(pq.at[r], size * bpd)
        for s in (-1, 1):
            @pl.when(exists(0, s))
            def _():
                for k in reversed(range(ngx)):
                    pltpu.make_async_remote_copy(
                        src_ref=pbuf.at[1, gx, ks], dst_ref=pbuf.at[1 - s, gx, ks], send_sem=ps.at[0],
                        recv_sem=pn.at[r, (1 - s) // 2], device_id={"gx": far(gx, k, ngx), "gy": gy + s},
                        device_id_type=MESH).start()

    def expand(d, k):
        u = jnp.zeros((rowblk, sblk), f32)
        for g in range(ngx):
            for l in range(bpd):
                u = u + jnp.where(block_f == pbuf[d, g, 1, l], pbuf[d, g, k, l], 0.0)
        return u

    def ring_fix(f, r, k, size):
        if ngx > 1:
            wait_rows(pr.at[r], (ngx - 1) * size * bpd)
        ub[1, 1 : 1 + rowblk] = expand(1, k).reshape(rowblk, 1, sblk)

        def row(d, j):
            return ub[d, gx * bpd + j]

        for l in range(bpd):
            take_off(f, l, to_full(row(1, 1 + l)))
        for j, x, at in ((0, 0, sblk - cy), (bpd + 1, cx + 1, 0)):
            col = jnp.sum(jnp.where(eye[at : at + cy], row(1, j), 0.0), axis=1, keepdims=True)
            f[last, x, YB : YB + cy, :] = f[last, x, YB : YB + cy, :] - jnp.where(lane_row == 0, col, 0.0)
        if r == 0:
            pass_on(1, 2, 1)
        for d, y, off in ((0, YB - 1, cy - 1), (2, YB + cy, 0)):
            pl.when(exists(0, d - 1))(lambda: wait_rows(pn.at[r, d // 2], ngx * size * bpd))
            ub[d, 1 : 1 + rowblk] = expand(d, k).reshape(rowblk, 1, sblk)
            for xi in range(cx + 2):
                j = (xi - 1 + per) // per
                at = ((xi - 1 + per) % per) * cy + off
                val = pltpu.roll(row(d, j), (nz - at) % nz, 1)
                f[last, xi, y : y + 1, :] = f[last, xi, y : y + 1, :] - jnp.where(lane_one == 0, val, 0.0)

    def planes(f, c, emit, first, stop):
        window = []
        for x in range(first, stop + 2):
            kap = [f0[comp, x, YB + s : YB + s + cy, :] for s in (-1, 0, 1)]
            val = [f[c, x, YB + s : YB + s + cy, :] for s in (-1, 0, 1)]
            window.append((val[1] + 0.5 * (val[0] + val[2]),
                           kap[1] * val[1] + 0.5 * (kap[0] * val[0] + kap[2] * val[2])))
            if len(window) >= 3:
                p = window[-2][0] + 0.5 * (window[-3][0] + window[-1][0])
                q = window[-2][1] + 0.5 * (window[-3][1] + window[-1][1])
                k0 = f0[comp, x - 1, YB : YB + cy, :]
                v0 = f[c, x - 1, YB : YB + cy, :]
                emit(c, x - 2, diag[x - 2] * v0 - k0 * tz(p) - tz(q))

    def apply(f, c, emit):
        planes(f, c, emit, 0, cx)

    def edges(f, c, emit):
        planes(f, c, emit, 0, 1)
        planes(f, c, emit, cx - 1, cx)

    def inside(f, c, emit):
        planes(f, c, emit, 1, cx - 1)

    def make_diag():
        window = []
        for x in range(cx + 2):
            kap = [f0[comp, x, YB + s : YB + s + cy, :] for s in (-1, 0, 1)]
            window.append(kap[1] + 0.5 * (kap[0] + kap[2]))
            if x >= 2:
                p = window[x - 1] + 0.5 * (window[x - 2] + window[x])
                diag[x - 2] = sigma_v[x - 2] + 8.0 * f0[comp, x - 1, YB : YB + cy, :] + tz(p)

    def emit_rhs(c, x, val):
        f1[c, 1 + x, YB : YB + cy, :] = force_v[c, x] - val

    def emit_v1(c, x, val):
        f2[c, 1 + x, YB : YB + cy, :] = val

    def traction(x):
        rows = slice((x % per) * cy, (x % per + 1) * cy)
        return jnp.where(lane_row == 0, t_f[x // per, rows, :], 0.0)

    def emit_rhs_t(c, x, val):
        f1[c, 1 + x, YB : YB + cy, :] = force_v[c, x] - val - traction(x)

    def emit_v1_t(c, x, val):
        f2[c, 1 + x, YB : YB + cy, :] = val - traction(x)

    def r0_of(c, x):
        return f1[c, 1 + x, YB : YB + cy, :]

    def v1_of(c, x):
        return f2[c, 1 + x, YB : YB + cy, :]

    def fold(v):
        return jnp.sum(v.reshape(cy // 8, 8, nz), axis=0)

    def gather(c, wanted, fields):
        sums = {}
        for x in range(cx):
            for k, (left, right) in wanted.items():
                term = fold(fields(x)[left] * fields(x)[right])
                sums[k] = sums[k] + term if k in sums else term
        for k, v in sums.items():
            acc[k] = acc[k] + v

    def dots(c):
        gather(c, {RR: (0, 0), RV: (0, 1), VV: (1, 1)}, lambda x: (r0_of(c, x), v1_of(c, x)))

    def total(v):
        return jnp.sum(jnp.sum(v, axis=0, keepdims=True), axis=1, keepdims=True)

    def choose_own():
        rv, vv = total(acc[RV]), total(acc[VV])
        own = jnp.where(vv > 0.0, rv / jnp.where(vv > 0.0, vv, 1.0), 0.0)
        own_ref[...] = jnp.broadcast_to(own, (cy, nz))

    def near_dots(c):
        own = own_ref[...]
        gather(c, {NN: (0, 0), NV: (0, 1)}, lambda x: (r0_of(c, x) - own * v1_of(c, x), v1_of(c, x)))

    def image_dots(c, more):
        own = own_ref[...]
        sums = {}

        def emit(c, x, val):
            v = v1_of(c, x)
            r = r0_of(c, x)
            near = r - own * v
            terms = {NW: near * val, VW: v * val}
            if more:
                terms.update({RV: r * v, VV: v * v, NN: near * near, NV: near * v})
            for k, t in terms.items():
                sums[k] = sums[k] + fold(t) if k in sums else fold(t)
        apply(f2, c, emit)
        for k, v in sums.items():
            acc[k] = acc[k] + v

    def first_comps(act):
        @pl.loop(0, last)
        def _(c):
            act(c)

    def gap_of(l, s1):
        picked = jnp.sum(jnp.where(block_of == partner[l], s1, 0.0), axis=0, keepdims=True)
        return base[l] - jnp.broadcast_to(jnp.sum(mort[l] * picked, axis=1, keepdims=True), (sblk, nz))

    def pull(l, k, t):
        pbuf[1, gx, k, l] = jnp.sum(mort[l] * t, axis=0, keepdims=True)

    def surf_rows(r):
        return s1b[r].reshape(rowblk, sblk)

    def send_final():
        sub = lax.broadcasted_iota(jnp.int32, (8, nz), 0)
        stack = jnp.zeros((8, nz), f32)
        for k in range(OWN):
            stack = jnp.where(sub == k, jnp.broadcast_to(jnp.sum(acc[k], axis=0, keepdims=True), (8, nz)), stack)
        lanes = lax.broadcasted_iota(jnp.int32, (8, nz), 1)
        stack = jnp.where((sub == OWN) & (lanes == 0), own_ref[0:8, :], stack)
        final[me] = jnp.sum(jnp.where(sub == lanes, jnp.sum(stack, axis=1, keepdims=True), 0.0), axis=0, keepdims=True)

        def go(place):
            pltpu.make_async_remote_copy(
                src_ref=final.at[me], dst_ref=final.at[me], send_sem=fin.at[0], recv_sem=fin.at[1],
                device_id=place, device_id_type=MESH).start()
        if count <= 64:
            for kx in reversed(range(ngx)):
                for ky in reversed(range(ngy)):
                    for kb in reversed(range(nb)):
                        if kx or ky or kb:
                            go({"body": far(b, kb, nb), "gx": far(gx, kx, ngx), "gy": far(gy, ky, ngy)})
        else:
            each_peer(lambda k: go(place_of(lax.rem(me + k, count))))

    pl.semaphore_wait(barrier, expect)
    halo_send_args(CORNERS + ALONG_Y)

    @pl.when(b == 1)
    def _():
        wait_rows(ls.at[0], cx * cy)
        surface_rows(f0, 0)
        surf_send(0)

    halo_send_args(FACES_X)

    @pl.when(b == 1)
    def _():
        wait_rows(ls.at[1], comp * cx * cy)
        wait_rows(ls.at[2], (comp + 1) * cx * cy)
        wait_halo(hr.at[0], comp + 1)
        make_diag()
        first_comps(lambda c: edges(f0, c, emit_rhs))
        halo_send(f1, 0, last, hs.at[0], hr.at[1], ACROSS_X)
        edges(f0, last, emit_rhs)
        halo_send(f1, last, 1, hs.at[1], hr.at[2], ACROSS_X)
        inside(f0, last, emit_rhs)
        surface_rows(f1, 1)
        surf_send(1)
        halo_send(f1, last, 1, hs.at[1], hr.at[2], ALONG_Y)
        pass_on(0, 0, 2)
        first_comps(lambda c: inside(f0, c, emit_rhs))
        halo_send(f1, 0, last, hs.at[0], hr.at[1], ALONG_Y)

        wait_halo(hr.at[1], last)
        first_comps(lambda c: edges(f1, c, emit_v1))
        halo_send(f2, 0, last, hs.at[0], hr.at[3], ACROSS_X)
        first_comps(lambda c: inside(f1, c, emit_v1))
        halo_send(f2, 0, last, hs.at[0], hr.at[3], ALONG_Y)
        wait_halo(hs.at[1], 1)
        wait_halo(hr.at[2], 1)
        ring_fix(f1, 0, 0, 2)
        edges(f1, last, emit_v1)
        halo_send(f2, last, 1, hs.at[2], hr.at[4], ACROSS_X)
        inside(f1, last, emit_v1)
        surface_rows(f2, 2)
        surf_send(2)
        halo_send(f2, last, 1, hs.at[2], hr.at[4], ALONG_Y)
        first_comps(dots)
        choose_own()
        first_comps(near_dots)
        gather(last, {RR: (0, 0)}, lambda x: (r0_of(last, x),))

        wait_halo(hr.at[3], last)
        first_comps(lambda c: image_dots(c, False))
        wait_halo(hs.at[2], 1)
        wait_halo(hr.at[4], 1)
        ring_fix(f2, 1, 2, 1)
        image_dots(last, True)
        send_final()

    @pl.when(b == 0)
    def _():
        for k in range(4):
            sem, rows = ((ls.at[0], cx * cy), (ls.at[3], 2 * bpd), (ls.at[6], bpd * sblk), (ls.at[1], comp * cx * cy))[k]
            wait_rows(sem, rows)
        pltpu.make_async_copy(partner_in, partner, ls.at[4]).wait()
        pltpu.make_async_copy(active_in, active, ls.at[5]).wait()
        for l in range(bpd):
            base[l] = to_full(gap0[l : l + 1, :]) - first_of(f0, l)
            prs_f[l] = to_full(press[l : l + 1, :])
            pbuf[1, gx, 1, l] = jnp.full((1, sblk), partner[l].astype(f32))
        wait_rows(sr.at[0], ngx * bpd)
        s1 = surf_rows(0)
        for l in range(bpd):
            gap = gap_of(l, s1)
            prs = prs_f[l]
            radius = jnp.sqrt(gap * gap + prs * prs + 0.01)
            per_radius = 1.0 / radius
            per_divisor = 1.0 / ((1.0 - prs * per_radius) + 0.5)
            flag = active[l].astype(f32)
            excess = (gap + prs - radius) * per_divisor
            slope = (1.0 - gap * per_radius) * per_divisor
            t = flag * (prs - excess)
            pull(l, 0, t)
            t_f[l] = t
            ex_f[l] = excess
            sl_f[l] = slope
            st_f[l] = flag * slope
        pulled_send(0, 2, 0)
        wait_rows(ls.at[2], (comp + 1) * cx * cy)
        wait_halo(hr.at[0], comp + 1)
        make_diag()
        first_comps(lambda c: edges(f0, c, emit_rhs))
        halo_send(f1, 0, last, hs.at[0], hr.at[1], ACROSS_X)
        edges(f0, last, emit_rhs_t)
        halo_send(f1, last, 1, hs.at[1], hr.at[2], ACROSS_X)
        first_comps(lambda c: inside(f0, c, emit_rhs))
        halo_send(f1, 0, last, hs.at[0], hr.at[1], ALONG_Y)
        inside(f0, last, emit_rhs_t)
        halo_send(f1, last, 1, hs.at[1], hr.at[2], ALONG_Y)
        for l in range(bpd):
            base[l] = -first_of(f1, l)

        wait_rows(sr.at[1], ngx * bpd)
        if ngx > 1:
            wait_rows(pr.at[0], (ngx - 1) * 2 * bpd)
        s1 = surf_rows(1) - expand(1, 0)
        for l in range(bpd):
            gap = gap_of(l, s1)
            t = st_f[l] * gap
            pull(l, 2, t)
            t_f[l] = t
            gr_f[l] = gap
        pulled_send(2, 1, 1)
        wait_halo(hr.at[1], last)
        first_comps(lambda c: edges(f1, c, emit_v1))
        halo_send(f2, 0, last, hs.at[0], hr.at[3], ACROSS_X)
        wait_halo(hr.at[2], 1)
        edges(f1, last, emit_v1_t)
        halo_send(f2, last, 1, hs.at[2], hr.at[4], ACROSS_X)
        first_comps(lambda c: inside(f1, c, emit_v1))
        halo_send(f2, 0, last, hs.at[0], hr.at[3], ALONG_Y)
        inside(f1, last, emit_v1_t)
        halo_send(f2, last, 1, hs.at[2], hr.at[4], ALONG_Y)
        for l in range(bpd):
            base[l] = -first_of(f2, l)
        first_comps(dots)
        choose_own()
        dots(last)
        pl.loop(0, comp)(near_dots)
        wait_halo(hr.at[3], last)
        first_comps(lambda c: image_dots(c, False))
        wait_halo(hr.at[4], 1)
        image_dots(last, False)

        wait_rows(sr.at[2], ngx * bpd)
        if ngx > 1:
            wait_rows(pr.at[1], (ngx - 1) * bpd)
        s1 = surf_rows(2) - expand(1, 2)
        own = own_ref[0:1, :]
        for l in range(bpd):
            gap = gap_of(l, s1)
            gv_f[l] = gap
            weighted = st_f[l] * gap
            for k, left in ((NW, gr_f[l] - own * gap), (VW, gap)):
                row = jnp.sum(weighted * left, axis=0, keepdims=True)
                acc[k, 0:1] = acc[k, 0:1] + jnp.where(lane_one == 0, row, 0.0)
        send_final()
        for l in range(bpd):
            flag = active[l].astype(f32)
            npr[0, l] = flag * (press[l : l + 1, :] - to_row(ex_f[l]))
            npr[1, l] = flag * to_row(sl_f[l] * gr_f[l])
            npr[2, l] = flag * to_row(sl_f[l] * gv_f[l])
        pltpu.make_async_remote_copy(src_ref=npr, dst_ref=npr, send_sem=nps.at[0], recv_sem=nps.at[1],
                                     device_id={"body": 1}, device_id_type=MESH).start()

    @pl.when(b == 1)
    def _():
        wait_rows(ls.at[3], 2 * bpd)
        wait_rows(ls.at[6], bpd * sblk)
        pltpu.make_async_copy(partner_in, partner, ls.at[4]).wait()
        pltpu.make_async_copy(active_in, active, ls.at[5]).wait()
        wait_rows(ss.at[0], 3 * ngx * bpd)
        for c in sides(ngy):
            if c:
                pl.when(nys == c)(lambda: wait_rows(ps.at[0], 3 * bpd * c * ngx))
        wait_rows(nps.at[1], 3 * bpd)

    @pl.when(b == 0)
    def _():
        wait_rows(ps.at[0], 3 * bpd * (2 * ngx - 1))
        wait_halo(hs.at[1], 1)
        wait_halo(hs.at[2], 1)
        wait_rows(nps.at[0], 3 * bpd)

    wait_halo(hs.at[0], comp + 1 + 2 * last)
    wait_rows(fin.at[0], count - 1)
    for c in range(comp):
        for x in range(cx):
            r0_out[c, x] = r0_of(c, x)
            v1_out[c, x] = v1_of(c, x)
    npr_out[...] = npr[...]

    wait_rows(fin.at[1], count - 1)
    table = final[...].reshape(count, sblk)
    lanes = lax.broadcasted_iota(jnp.int32, (count, sblk), 1)
    sums = jnp.sum(table, axis=0, keepdims=True)
    norm0 = sums[:, RR : RR + 1]
    alpha0 = norm0 / sums[:, RV : RV + 1]
    delta = alpha0 - table[:, OWN : OWN + 1]

    def pick(weights):
        w = jnp.zeros((count, sblk), f32)
        for k, v in weights:
            w = jnp.where(lanes == k, v, w)
        return total(w * table)

    norm1 = pick(((NN, 1.0), (NV, -2.0 * delta), (VV, delta * delta)))
    product1 = pick(((NV, 1.0), (VV, -delta), (NW, -alpha0), (VW, alpha0 * delta)))
    ratio = norm1 / norm0
    alpha1 = norm1 / (product1 - ratio * norm1 / alpha0)
    coef[0:1, :] = jnp.broadcast_to(alpha0 + alpha1 * (1.0 + ratio), (1, nz))
    coef[1:2, :] = jnp.broadcast_to(-alpha1 * alpha0, (1, nz))


def out_kernel(r0, v1, coef, npr, inc, new_press, buf, rows, sems):
    comp, cx, cy, nz = buf.shape
    bpd = rows.shape[0]
    cr, cv = coef[0:1, :], coef[1:2, :]
    copies = []
    for c in range(comp):
        for x in range(cx):
            buf[c, x] = cr * r0[c, x] + cv * v1[c, x]
        copies.append(pltpu.make_async_copy(buf.at[c], inc.at[0, c], sems.at[c]))
        copies[-1].start()
    for l in range(bpd):
        rows[l : l + 1, :] = npr[0, l] - (cr * npr[1, l] + cv * npr[2, l])
    copies.append(pltpu.make_async_copy(rows, new_press, sems.at[comp]))
    copies[-1].start()
    for copy in copies:
        copy.wait()


def on_device(disp, force, kappa, sigma, gap0, pressure, mortar, partner, active):
    nb, ngx, ngy = (lax.axis_size(a) for a in ("body", "gx", "gy"))
    _, comp, cx, cy, nz = disp.shape
    bpd, sblk, _ = mortar.shape
    f32 = jnp.float32
    any_spec = pl.BlockSpec(memory_space=pl.ANY)
    vmem = pl.BlockSpec(memory_space=pltpu.VMEM)
    rows = cy + 2 * YB
    rowblk = ngx * bpd
    count = nb * ngx * ngy
    dma = pltpu.SemaphoreType.DMA
    full = pltpu.VMEM((bpd, sblk, nz), f32)
    most = max((comp + 1) * cx * cy, (comp + 1 + 2 * (comp - 1)) * 2 * (cy + cx + 2), count, bpd * sblk,
               3 * bpd * 4 * ngx)
    field = (comp, cx + 2, rows, nz)
    r0, v1, coef, npr = pl.pallas_call(
        functools.partial(kernel, nb, ngx, ngy),
        out_shape=(pltpu.VMEM((comp, cx, cy, nz), f32), pltpu.VMEM((comp, cx, cy, nz), f32), pltpu.VMEM((8, nz), f32),
                   pltpu.VMEM((3, bpd, 1, sblk), f32)),
        in_specs=[any_spec] * 9,
        out_specs=(vmem,) * 4,
        scratch_shapes=[
            pltpu.VMEM((bpd, sblk), f32),
            pltpu.VMEM((bpd, sblk), f32),
            pltpu.SMEM((bpd,), jnp.int32),
            pltpu.SMEM((bpd,), jnp.int32),
            pltpu.VMEM((comp + 1, cx + 2, rows, nz), f32),
            pltpu.VMEM(field, f32),
            pltpu.VMEM(field, f32),
            pltpu.VMEM((3, bpd, 1, sblk), f32),
            pltpu.VMEM((cx, cy, nz), f32),
            pltpu.VMEM((comp, cx, cy, nz), f32),
            pltpu.VMEM((cx, cy, nz), f32),
            pltpu.VMEM((bpd, sblk, sblk), f32),
            pltpu.VMEM((3, ngx, bpd, 1, sblk), f32),
            pltpu.VMEM((3, ngx, 3, bpd, 1, sblk), f32),
            pltpu.VMEM((3, rowblk + 2, 1, sblk), f32),
            full, full, full, full, full, full, full, full,
            pltpu.VMEM((8, 8, nz), f32),
            pltpu.VMEM((cy, nz), f32),
            pltpu.VMEM((count, 1, sblk), f32),
            pltpu.VMEM((most, 1, nz), f32),
            dma((7,)), dma((5,)), dma((3,)), dma((3,)), dma((1,)), dma((2,)), dma((2,)), dma((2, 2)), dma((1,)), dma((2,)),
            dma((2,)),
        ],
        compiler_params=pltpu.CompilerParams(collective_id=0, has_side_effects=True,
                                             vmem_limit_bytes=60 * 1024 * 1024),
        name="newton_step",
    )(disp, force, kappa, sigma, gap0, pressure, mortar, partner, active)
    return pl.pallas_call(
        out_kernel,
        out_shape=(jax.ShapeDtypeStruct(disp.shape, f32), jax.ShapeDtypeStruct(gap0.shape, f32)),
        in_specs=[vmem] * 4,
        out_specs=(any_spec, any_spec),
        scratch_shapes=[pltpu.VMEM((comp, cx, cy, nz), f32), pltpu.VMEM((bpd, sblk), f32), dma((comp + 1,))],
        compiler_params=pltpu.CompilerParams(vmem_limit_bytes=4 * 1024 * 1024),
        name="newton_out",
    )(r0, v1, coef, npr)


def solution(mesh):
    placed = (
        P("body", None, "gx", "gy", None),
        P("body", None, "gx", "gy", None),
        P("body", "gx", "gy", None),
        P("body", "gx", "gy", None),
        P(("gx", "gy"), None),
        P(("gx", "gy"), None),
        P(("gx", "gy"), None, None),
        P(("gx", "gy")),
        P(("gx", "gy")),
    )
    return jax.shard_map(
        on_device,
        mesh=mesh,
        in_specs=placed,
        out_specs=(P("body", None, "gx", "gy", None), P(("gx", "gy"), None)),
        check_vma=False,
    )
```

```python
import functools

import jax
import jax.numpy as jnp
from jax import lax
from jax.experimental import pallas as pl
from jax.experimental.pallas import tpu as pltpu
from jax.sharding import PartitionSpec as P

MESH = pl.DeviceIdType.MESH
YB = 8
CORNERS = tuple((dx, dy) for dx in (-1, 1) for dy in (-1, 1))
ALONG_Y = ((0, -1), (0, 1))
ACROSS_X = CORNERS + ((-1, 0), (1, 0))
FACES_X = ((-1, 0), (1, 0))
DIRS = CORNERS + ALONG_Y + FACES_X
RR, RV, VV, NN, NV, NW, VW, OWN = range(8)


def kernel(nb, ngx, ngy, disp, force, kappa, sigma, gap0_in, press_in, mortar, partner_in, active_in,
           r0_out, v1_out, coef, npr_out,
           gap0, press, partner, active, f0, f1, f2, npr, diag, force_v, sigma_v, mort, s1b, pbuf, ub, base, prs_f, t_f, ex_f, sl_f,
           st_f, gr_f, gv_f, acc, own_ref, final, dummy,
           ls, hr, hs, sr, ss, pr, pq, pn, ps, nps, fin):
    comp, cx, cy, nz = force_v.shape
    bpd, sblk = gap0.shape
    per = sblk // cy
    rowblk = ngx * bpd
    last = comp - 1
    b = lax.axis_index("body")
    gx = lax.axis_index("gx")
    gy = lax.axis_index("gy")
    count = nb * ngx * ngy
    me = (b * ngx + gx) * ngy + gy
    f32 = jnp.float32

    def far(at, k, size):
        if size & (size - 1):
            return lax.rem(at + k, size)
        for bit in (1 << i for i in range(size.bit_length() - 1)):
            if k & bit:
                at = at + bit - 2 * bit * lax.rem(at // bit, 2)
        return at

    def place_of(other):
        return {"body": other // (ngx * ngy), "gx": lax.rem(other // ngy, ngx), "gy": lax.rem(other, ngy)}

    def each_peer(act):
        if count <= 64:
            for k in range(1, count):
                act(k)
        else:
            pl.loop(1, count)(act)

    def exists(dx, dy):
        good = jnp.bool_(True)
        if dx < 0:
            good = good & (gx >= 1)
        if dx > 0:
            good = good & (gx < ngx - 1)
        if dy < 0:
            good = good & (gy >= 1)
        if dy > 0:
            good = good & (gy < ngy - 1)
        return good

    def as_int(flag):
        return flag.astype(jnp.int32)

    nys = as_int(exists(0, -1)) + as_int(exists(0, 1))
    nxs = as_int(exists(-1, 0)) + as_int(exists(1, 0))

    def sides(size):
        return (0,) if size == 1 else (1,) if size == 2 else (1, 2)

    def wait_rows(sem, rows):
        part = dummy.at[pl.ds(0, rows)]
        pltpu.make_async_copy(part, part, sem).wait()

    def wait_halo(sem, comps):
        for a in sides(ngx):
            for c in sides(ngy):
                rows = comps * (a * cy + c * cx + a * c)
                if rows:
                    pl.when((nxs == a) & (nys == c))(lambda: wait_rows(sem, rows))

    barrier = pltpu.get_barrier_semaphore()
    if ngy <= 4:
        expect = jnp.where(b == 1, ngx, 0)
        for dx, dy in DIRS:
            here = exists(dx, dy)
            expect = expect + as_int(here)

            @pl.when(here)
            def _():
                pl.semaphore_signal(barrier, inc=1, device_id={"gx": gx + dx, "gy": gy + dy}, device_id_type=MESH)
        for g in range(ngx):
            @pl.when(b == 0)
            def _():
                pl.semaphore_signal(barrier, inc=1, device_id={"body": 1, "gx": g}, device_id_type=MESH)
    else:
        each_peer(lambda k: pl.semaphore_signal(barrier, inc=1, device_id=place_of(lax.rem(me + k, count)),
                                                device_id_type=MESH))
        expect = count - 1

    inner = (pl.ds(1, cx), pl.ds(YB, cy))
    pltpu.make_async_copy(disp.at[0, last], f0.at[(last,) + inner], ls.at[0]).start()
    pltpu.make_async_copy(disp.at[0, pl.ds(0, last)], f0.at[(pl.ds(0, last),) + inner], ls.at[1]).start()
    pltpu.make_async_copy(kappa.at[0], f0.at[(comp,) + inner], ls.at[1]).start()
    pltpu.make_async_copy(gap0_in, gap0, ls.at[3]).start()
    pltpu.make_async_copy(press_in, press, ls.at[3]).start()
    pltpu.make_async_copy(partner_in, partner, ls.at[4]).start()
    pltpu.make_async_copy(active_in, active, ls.at[5]).start()
    pltpu.make_async_copy(mortar, mort, ls.at[6]).start()
    pltpu.make_async_copy(sigma.at[0], sigma_v, ls.at[2]).start()
    pltpu.make_async_copy(force.at[0], force_v, ls.at[2]).start()

    for side, x in ((-1, 0), (1, cx + 1)):
        @pl.when(jnp.logical_not(exists(side, 0)))
        def _():
            for f in (f0, f1, f2):
                for c in range(f.shape[0]):
                    f[c, x, YB - 1 : YB] = jnp.zeros((1, nz), f32)
                    f[c, x, YB : YB + cy] = jnp.zeros((cy, nz), f32)
                    f[c, x, YB + cy : YB + cy + 1] = jnp.zeros((1, nz), f32)
    for side, y in ((-1, YB - 1), (1, YB + cy)):
        @pl.when(jnp.logical_not(exists(0, side)))
        def _():
            for f in (f0, f1, f2):
                for c in range(f.shape[0]):
                    for x in range(cx + 2):
                        f[c, x, y : y + 1] = jnp.zeros((1, nz), f32)
            for g in range(ngx):
                for k in range(3):
                    for l in range(bpd):
                        pbuf[1 + side, g, k, l] = jnp.zeros((1, sblk), f32)
    for d in range(3):
        for q in (0, rowblk + 1):
            ub[d, q] = jnp.zeros((1, sblk), f32)
    for k in range(8):
        acc[k] = jnp.zeros((8, nz), f32)

    lane = lax.broadcasted_iota(jnp.int32, (sblk, nz), 1)
    eye = lax.broadcasted_iota(jnp.int32, (sblk, nz), 0) == lane
    first_lane = lane == 0
    lane_row = lax.broadcasted_iota(jnp.int32, (cy, nz), 1)
    left_w = jnp.where(lane_row == 0, 0.0, 0.5)
    right_w = jnp.where(lane_row == nz - 1, 0.0, 0.5)
    lane_one = lax.broadcasted_iota(jnp.int32, (1, nz), 1)
    block_of = lax.broadcasted_iota(jnp.int32, (rowblk, sblk), 0)
    block_f = block_of.astype(f32)

    def to_full(row):
        return jnp.broadcast_to(jnp.sum(jnp.where(eye, row, 0.0), axis=1, keepdims=True), (sblk, nz))

    def to_row(full):
        return jnp.sum(jnp.where(eye, full, 0.0), axis=0, keepdims=True)

    def tz(v):
        return v + left_w * pltpu.roll(v, 1, 1) + right_w * pltpu.roll(v, nz - 1, 1)

    def block(f, l):
        return f[last, 1 + l * per : 1 + (l + 1) * per, YB : YB + cy, :].reshape(sblk, nz)

    def first_of(f, l):
        return jnp.broadcast_to(block(f, l)[:, 0:1], (sblk, nz))

    def take_off(f, l, full):
        xs = slice(1 + l * per, 1 + (l + 1) * per)
        f[last, xs, YB : YB + cy, :] = (block(f, l) - jnp.where(first_lane, full, 0.0)).reshape(per, cy, nz)

    def part(delta, size, base_at, src_base):
        if delta == 0:
            return pl.ds(src_base, size), pl.ds(base_at, size)
        if delta < 0:
            return pl.ds(src_base, 1), pl.ds(base_at + size, 1)
        return pl.ds(src_base + size - 1, 1), pl.ds(base_at - 1, 1)

    def halo_send(f, at, size, send_sem, recv_sem, dirs):
        cs = pl.ds(at, size)
        for dx, dy in dirs:
            @pl.when(exists(dx, dy))
            def _():
                sx, tx = part(dx, cx, 1, 1)
                sy, ty = part(dy, cy, YB, YB)
                pltpu.make_async_remote_copy(
                    src_ref=f.at[cs, sx, sy], dst_ref=f.at[cs, tx, ty], send_sem=send_sem, recv_sem=recv_sem,
                    device_id={"gx": gx + dx, "gy": gy + dy}, device_id_type=MESH).start()

    def halo_send_args(dirs):
        for dx, dy in dirs:
            @pl.when(exists(dx, dy))
            def _():
                sx, tx = part(dx, cx, 1, 0)
                sy, ty = part(dy, cy, YB, 0)
                for src, dst in ((disp.at[0, :, sx, sy], f0.at[pl.ds(0, comp), tx, ty]),
                                 (kappa.at[:, sx, sy], f0.at[pl.ds(comp, 1), tx, ty])):
                    pltpu.make_async_remote_copy(
                        src_ref=src, dst_ref=dst, send_sem=hs.at[0], recv_sem=hr.at[0],
                        device_id={"gx": gx + dx, "gy": gy + dy}, device_id_type=MESH).start()

    def surf_send(r):
        for k in reversed(range(ngx)):
            pltpu.make_async_remote_copy(
                src_ref=s1b.at[r, gx], dst_ref=s1b.at[r, gx], send_sem=ss.at[0], recv_sem=sr.at[r],
                device_id={"body": 0, "gx": far(gx, k, ngx)}, device_id_type=MESH).start()

    def surface_rows(f, r):
        for l in range(bpd):
            s1b[r, gx, l] = to_row(first_of(f, l))

    def pulled_send(first, size, r):
        ks = pl.ds(first, size)

        def go(bo, g, sem):
            pltpu.make_async_remote_copy(
                src_ref=pbuf.at[1, gx, ks], dst_ref=pbuf.at[1, gx, ks], send_sem=ps.at[0], recv_sem=sem,
                device_id={"body": bo, "gx": g}, device_id_type=MESH).start()
        go(1, gx, pq.at[r])
        for k in reversed(range(1, ngx)):
            go(1, far(gx, k, ngx), pr.at[r])
            go(0, far(gx, k, ngx), pr.at[r])

    def pass_on(r, first, size):
        ks = pl.ds(first, size)
        wait_rows(pq.at[r], size * bpd)
        for s in (-1, 1):
            @pl.when(exists(0, s))
            def _():
                for k in reversed(range(ngx)):
                    pltpu.make_async_remote_copy(
                        src_ref=pbuf.at[1, gx, ks], dst_ref=pbuf.at[1 - s, gx, ks], send_sem=ps.at[0],
                        recv_sem=pn.at[r, (1 - s) // 2], device_id={"gx": far(gx, k, ngx), "gy": gy + s},
                        device_id_type=MESH).start()

    def expand(d, k):
        u = jnp.zeros((rowblk, sblk), f32)
        for g in range(ngx):
            for l in range(bpd):
                u = u + jnp.where(block_f == pbuf[d, g, 1, l], pbuf[d, g, k, l], 0.0)
        return u

    def ring_fix(f, r, k, size):
        if ngx > 1:
            wait_rows(pr.at[r], (ngx - 1) * size * bpd)
        ub[1, 1 : 1 + rowblk] = expand(1, k).reshape(rowblk, 1, sblk)

        def row(d, j):
            return ub[d, gx * bpd + j]

        for l in range(bpd):
            take_off(f, l, to_full(row(1, 1 + l)))
        for j, x, at in ((0, 0, sblk - cy), (bpd + 1, cx + 1, 0)):
            col = jnp.sum(jnp.where(eye[at : at + cy], row(1, j), 0.0), axis=1, keepdims=True)
            f[last, x, YB : YB + cy, :] = f[last, x, YB : YB + cy, :] - jnp.where(lane_row == 0, col, 0.0)
        if r == 0:
            pass_on(1, 2, 1)
        for d, y, off in ((0, YB - 1, cy - 1), (2, YB + cy, 0)):
            pl.when(exists(0, d - 1))(lambda: wait_rows(pn.at[r, d // 2], ngx * size * bpd))
            ub[d, 1 : 1 + rowblk] = expand(d, k).reshape(rowblk, 1, sblk)
            for xi in range(cx + 2):
                j = (xi - 1 + per) // per
                at = ((xi - 1 + per) % per) * cy + off
                val = pltpu.roll(row(d, j), (nz - at) % nz, 1)
                f[last, xi, y : y + 1, :] = f[last, xi, y : y + 1, :] - jnp.where(lane_one == 0, val, 0.0)

    def planes(f, c, emit, first, stop):
        window = []
        for x in range(first, stop + 2):
            kap = [f0[comp, x, YB + s : YB + s + cy, :] for s in (-1, 0, 1)]
            val = [f[c, x, YB + s : YB + s + cy, :] for s in (-1, 0, 1)]
            window.append((val[1] + 0.5 * (val[0] + val[2]),
                           kap[1] * val[1] + 0.5 * (kap[0] * val[0] + kap[2] * val[2])))
            if len(window) >= 3:
                p = window[-2][0] + 0.5 * (window[-3][0] + window[-1][0])
                q = window[-2][1] + 0.5 * (window[-3][1] + window[-1][1])
                k0 = f0[comp, x - 1, YB : YB + cy, :]
                v0 = f[c, x - 1, YB : YB + cy, :]
                emit(c, x - 2, diag[x - 2] * v0 - k0 * tz(p) - tz(q))

    def apply(f, c, emit):
        planes(f, c, emit, 0, cx)

    def edges(f, c, emit):
        planes(f, c, emit, 0, 1)
        planes(f, c, emit, cx - 1, cx)

    def inside(f, c, emit):
        planes(f, c, emit, 1, cx - 1)

    def make_diag():
        window = []
        for x in range(cx + 2):
            kap = [f0[comp, x, YB + s : YB + s + cy, :] for s in (-1, 0, 1)]
            window.append(kap[1] + 0.5 * (kap[0] + kap[2]))
            if x >= 2:
                p = window[x - 1] + 0.5 * (window[x - 2] + window[x])
                diag[x - 2] = sigma_v[x - 2] + 8.0 * f0[comp, x - 1, YB : YB + cy, :] + tz(p)

    def emit_rhs(c, x, val):
        f1[c, 1 + x, YB : YB + cy, :] = force_v[c, x] - val

    def emit_v1(c, x, val):
        f2[c, 1 + x, YB : YB + cy, :] = val

    def traction(x):
        rows = slice((x % per) * cy, (x % per + 1) * cy)
        return jnp.where(lane_row == 0, t_f[x // per, rows, :], 0.0)

    def emit_rhs_t(c, x, val):
        f1[c, 1 + x, YB : YB + cy, :] = force_v[c, x] - val - traction(x)

    def emit_v1_t(c, x, val):
        f2[c, 1 + x, YB : YB + cy, :] = val - traction(x)

    def r0_of(c, x):
        return f1[c, 1 + x, YB : YB + cy, :]

    def v1_of(c, x):
        return f2[c, 1 + x, YB : YB + cy, :]

    def fold(v):
        return jnp.sum(v.reshape(cy // 8, 8, nz), axis=0)

    def gather(c, wanted, fields):
        sums = {}
        for x in range(cx):
            for k, (left, right) in wanted.items():
                term = fold(fields(x)[left] * fields(x)[right])
                sums[k] = sums[k] + term if k in sums else term
        for k, v in sums.items():
            acc[k] = acc[k] + v

    def dots(c):
        gather(c, {RR: (0, 0), RV: (0, 1), VV: (1, 1)}, lambda x: (r0_of(c, x), v1_of(c, x)))

    def total(v):
        return jnp.sum(jnp.sum(v, axis=0, keepdims=True), axis=1, keepdims=True)

    def choose_own():
        rv, vv = total(acc[RV]), total(acc[VV])
        own = jnp.where(vv > 0.0, rv / jnp.where(vv > 0.0, vv, 1.0), 0.0)
        own_ref[...] = jnp.broadcast_to(own, (cy, nz))

    def near_dots(c):
        own = own_ref[...]
        gather(c, {NN: (0, 0), NV: (0, 1)}, lambda x: (r0_of(c, x) - own * v1_of(c, x), v1_of(c, x)))

    def image_dots(c, more):
        own = own_ref[...]
        sums = {}

        def emit(c, x, val):
            v = v1_of(c, x)
            r = r0_of(c, x)
            near = r - own * v
            terms = {NW: near * val, VW: v * val}
            if more:
                terms.update({RV: r * v, VV: v * v, NN: near * near, NV: near * v})
            for k, t in terms.items():
                sums[k] = sums[k] + fold(t) if k in sums else fold(t)
        apply(f2, c, emit)
        for k, v in sums.items():
            acc[k] = acc[k] + v

    def first_comps(act):
        @pl.loop(0, last)
        def _(c):
            act(c)

    def gap_of(l, s1):
        picked = jnp.sum(jnp.where(block_of == partner[l], s1, 0.0), axis=0, keepdims=True)
        return base[l] - jnp.broadcast_to(jnp.sum(mort[l] * picked, axis=1, keepdims=True), (sblk, nz))

    def pull(l, k, t):
        pbuf[1, gx, k, l] = jnp.sum(mort[l] * t, axis=0, keepdims=True)

    def surf_rows(r):
        return s1b[r].reshape(rowblk, sblk)

    def send_final():
        sub = lax.broadcasted_iota(jnp.int32, (8, nz), 0)
        stack = jnp.zeros((8, nz), f32)
        for k in range(OWN):
            stack = jnp.where(sub == k, jnp.broadcast_to(jnp.sum(acc[k], axis=0, keepdims=True), (8, nz)), stack)
        lanes = lax.broadcasted_iota(jnp.int32, (8, nz), 1)
        stack = jnp.where((sub == OWN) & (lanes == 0), own_ref[0:8, :], stack)
        final[me] = jnp.sum(jnp.where(sub == lanes, jnp.sum(stack, axis=1, keepdims=True), 0.0), axis=0, keepdims=True)

        def go(place):
            pltpu.make_async_remote_copy(
                src_ref=final.at[me], dst_ref=final.at[me], send_sem=fin.at[0], recv_sem=fin.at[1],
                device_id=place, device_id_type=MESH).start()
        if count <= 64:
            for kx in reversed(range(ngx)):
                for ky in reversed(range(ngy)):
                    for kb in reversed(range(nb)):
                        if kx or ky or kb:
                            go({"body": far(b, kb, nb), "gx": far(gx, kx, ngx), "gy": far(gy, ky, ngy)})
        else:
            each_peer(lambda k: go(place_of(lax.rem(me + k, count))))

    def first_surface():
        wait_rows(ls.at[0], cx * cy)
        surface_rows(f0, 0)

    pl.when((b == 1) & (gx < ngx - 1))(first_surface)
    pl.semaphore_wait(barrier, expect)
    halo_send_args(CORNERS + ALONG_Y)

    @pl.when(b == 1)
    def _():
        pl.when(gx == ngx - 1)(first_surface)
        surf_send(0)

    halo_send_args(FACES_X)

    @pl.when(b == 1)
    def _():
        wait_rows(ls.at[1], comp * cx * cy)
        wait_rows(ls.at[2], (comp + 1) * cx * cy)
        wait_halo(hr.at[0], comp + 1)
        make_diag()
        first_comps(lambda c: edges(f0, c, emit_rhs))
        halo_send(f1, 0, last, hs.at[0], hr.at[1], ACROSS_X)
        edges(f0, last, emit_rhs)
        halo_send(f1, last, 1, hs.at[1], hr.at[2], ACROSS_X)
        inside(f0, last, emit_rhs)
        surface_rows(f1, 1)
        surf_send(1)
        halo_send(f1, last, 1, hs.at[1], hr.at[2], ALONG_Y)
        pass_on(0, 0, 2)
        first_comps(lambda c: inside(f0, c, emit_rhs))
        halo_send(f1, 0, last, hs.at[0], hr.at[1], ALONG_Y)

        wait_halo(hr.at[1], last)
        first_comps(lambda c: edges(f1, c, emit_v1))
        halo_send(f2, 0, last, hs.at[0], hr.at[3], ACROSS_X)
        first_comps(lambda c: inside(f1, c, emit_v1))
        halo_send(f2, 0, last, hs.at[0], hr.at[3], ALONG_Y)
        wait_halo(hs.at[1], 1)
        wait_halo(hr.at[2], 1)
        ring_fix(f1, 0, 0, 2)
        edges(f1, last, emit_v1)
        halo_send(f2, last, 1, hs.at[2], hr.at[4], ACROSS_X)
        inside(f1, last, emit_v1)
        surface_rows(f2, 2)
        surf_send(2)
        halo_send(f2, last, 1, hs.at[2], hr.at[4], ALONG_Y)
        first_comps(dots)
        choose_own()
        first_comps(near_dots)
        gather(last, {RR: (0, 0)}, lambda x: (r0_of(last, x),))

        wait_halo(hr.at[3], last)
        first_comps(lambda c: image_dots(c, False))
        wait_halo(hs.at[2], 1)
        wait_halo(hr.at[4], 1)
        ring_fix(f2, 1, 2, 1)
        image_dots(last, True)
        send_final()

    @pl.when(b == 0)
    def _():
        for k in range(4):
            sem, rows = ((ls.at[0], cx * cy), (ls.at[3], 2 * bpd), (ls.at[6], bpd * sblk), (ls.at[1], comp * cx * cy))[k]
            wait_rows(sem, rows)
        pltpu.make_async_copy(partner_in, partner, ls.at[4]).wait()
        pltpu.make_async_copy(active_in, active, ls.at[5]).wait()
        for l in range(bpd):
            base[l] = to_full(gap0[l : l + 1, :]) - first_of(f0, l)
            prs_f[l] = to_full(press[l : l + 1, :])
            pbuf[1, gx, 1, l] = jnp.full((1, sblk), partner[l].astype(f32))
        wait_rows(sr.at[0], ngx * bpd)
        s1 = surf_rows(0)
        for l in range(bpd):
            gap = gap_of(l, s1)
            prs = prs_f[l]
            radius = jnp.sqrt(gap * gap + prs * prs + 0.01)
            per_radius = 1.0 / radius
            per_divisor = 1.0 / ((1.0 - prs * per_radius) + 0.5)
            flag = active[l].astype(f32)
            excess = (gap + prs - radius) * per_divisor
            slope = (1.0 - gap * per_radius) * per_divisor
            t = flag * (prs - excess)
            pull(l, 0, t)
            t_f[l] = t
            ex_f[l] = excess
            sl_f[l] = slope
            st_f[l] = flag * slope
        pulled_send(0, 2, 0)
        wait_rows(ls.at[2], (comp + 1) * cx * cy)
        wait_halo(hr.at[0], comp + 1)
        make_diag()
        first_comps(lambda c: edges(f0, c, emit_rhs))
        halo_send(f1, 0, last, hs.at[0], hr.at[1], ACROSS_X)
        edges(f0, last, emit_rhs_t)
        halo_send(f1, last, 1, hs.at[1], hr.at[2], ACROSS_X)
        first_comps(lambda c: inside(f0, c, emit_rhs))
        halo_send(f1, 0, last, hs.at[0], hr.at[1], ALONG_Y)
        inside(f0, last, emit_rhs_t)
        halo_send(f1, last, 1, hs.at[1], hr.at[2], ALONG_Y)
        for l in range(bpd):
            base[l] = -first_of(f1, l)

        wait_rows(sr.at[1], ngx * bpd)
        if ngx > 1:
            wait_rows(pr.at[0], (ngx - 1) * 2 * bpd)
        s1 = surf_rows(1) - expand(1, 0)
        for l in range(bpd):
            gap = gap_of(l, s1)
            t = st_f[l] * gap
            pull(l, 2, t)
            t_f[l] = t
            gr_f[l] = gap
        pulled_send(2, 1, 1)
        wait_halo(hr.at[1], last)
        first_comps(lambda c: edges(f1, c, emit_v1))
        halo_send(f2, 0, last, hs.at[0], hr.at[3], ACROSS_X)
        wait_halo(hr.at[2], 1)
        edges(f1, last, emit_v1_t)
        halo_send(f2, last, 1, hs.at[2], hr.at[4], ACROSS_X)
        first_comps(lambda c: inside(f1, c, emit_v1))
        halo_send(f2, 0, last, hs.at[0], hr.at[3], ALONG_Y)
        inside(f1, last, emit_v1_t)
        halo_send(f2, last, 1, hs.at[2], hr.at[4], ALONG_Y)
        for l in range(bpd):
            base[l] = -first_of(f2, l)
        first_comps(dots)
        choose_own()
        dots(last)
        pl.loop(0, comp)(near_dots)
        wait_halo(hr.at[3], last)
        first_comps(lambda c: image_dots(c, False))
        wait_halo(hr.at[4], 1)
        image_dots(last, False)

        wait_rows(sr.at[2], ngx * bpd)
        if ngx > 1:
            wait_rows(pr.at[1], (ngx - 1) * bpd)
        s1 = surf_rows(2) - expand(1, 2)
        own = own_ref[0:1, :]
        for l in range(bpd):
            gap = gap_of(l, s1)
            gv_f[l] = gap
            weighted = st_f[l] * gap
            for k, left in ((NW, gr_f[l] - own * gap), (VW, gap)):
                row = jnp.sum(weighted * left, axis=0, keepdims=True)
                acc[k, 0:1] = acc[k, 0:1] + jnp.where(lane_one == 0, row, 0.0)
        send_final()
        for l in range(bpd):
            flag = active[l].astype(f32)
            npr[0, l] = flag * (press[l : l + 1, :] - to_row(ex_f[l]))
            npr[1, l] = flag * to_row(sl_f[l] * gr_f[l])
            npr[2, l] = flag * to_row(sl_f[l] * gv_f[l])
        pltpu.make_async_remote_copy(src_ref=npr, dst_ref=npr, send_sem=nps.at[0], recv_sem=nps.at[1],
                                     device_id={"body": 1}, device_id_type=MESH).start()

    @pl.when(b == 1)
    def _():
        wait_rows(ls.at[3], 2 * bpd)
        wait_rows(ls.at[6], bpd * sblk)
        pltpu.make_async_copy(partner_in, partner, ls.at[4]).wait()
        pltpu.make_async_copy(active_in, active, ls.at[5]).wait()
        wait_rows(ss.at[0], 3 * ngx * bpd)
        for c in sides(ngy):
            if c:
                pl.when(nys == c)(lambda: wait_rows(ps.at[0], 3 * bpd * c * ngx))
        wait_rows(nps.at[1], 3 * bpd)

    @pl.when(b == 0)
    def _():
        wait_rows(ps.at[0], 3 * bpd * (2 * ngx - 1))
        wait_halo(hs.at[1], 1)
        wait_halo(hs.at[2], 1)
        wait_rows(nps.at[0], 3 * bpd)

    wait_halo(hs.at[0], comp + 1 + 2 * last)
    wait_rows(fin.at[0], count - 1)
    for c in range(comp):
        for x in range(cx):
            r0_out[c, x] = r0_of(c, x)
            v1_out[c, x] = v1_of(c, x)
    npr_out[...] = npr[...]

    wait_rows(fin.at[1], count - 1)
    table = final[...].reshape(count, sblk)
    lanes = lax.broadcasted_iota(jnp.int32, (count, sblk), 1)
    sums = jnp.sum(table, axis=0, keepdims=True)
    norm0 = sums[:, RR : RR + 1]
    product0 = sums[:, RV : RV + 1]
    alpha0 = norm0 / product0
    per_norm0 = 1.0 / norm0
    delta = alpha0 - table[:, OWN : OWN + 1]

    def pick(weights):
        w = jnp.zeros((count, sblk), f32)
        for k, v in weights:
            w = jnp.where(lanes == k, v, w)
        return total(w * table)

    norm1 = pick(((NN, 1.0), (NV, -2.0 * delta), (VV, delta * delta)))
    product1 = pick(((NV, 1.0), (VV, -delta), (NW, -alpha0), (VW, alpha0 * delta)))
    ratio = norm1 * per_norm0
    alpha1 = norm1 / (product1 - ratio * (ratio * product0))
    coef[0:1, :] = jnp.broadcast_to(alpha0 + alpha1 * (1.0 + ratio), (1, nz))
    coef[1:2, :] = jnp.broadcast_to(-alpha1 * alpha0, (1, nz))


def out_kernel(r0, v1, coef, npr, inc, new_press, buf, rows, sems):
    comp, cx, cy, nz = buf.shape
    bpd = rows.shape[0]
    cr, cv = coef[0:1, :], coef[1:2, :]
    copies = []
    for l in range(bpd):
        rows[l : l + 1, :] = npr[0, l] - (cr * npr[1, l] + cv * npr[2, l])
    copies.append(pltpu.make_async_copy(rows, new_press, sems.at[comp]))
    copies[-1].start()
    for c in range(comp):
        for x in range(cx):
            buf[c, x] = cr * r0[c, x] + cv * v1[c, x]
        copies.append(pltpu.make_async_copy(buf.at[c], inc.at[0, c], sems.at[c]))
        copies[-1].start()
    for copy in copies:
        copy.wait()


def on_device(disp, force, kappa, sigma, gap0, pressure, mortar, partner, active):
    nb, ngx, ngy = (lax.axis_size(a) for a in ("body", "gx", "gy"))
    _, comp, cx, cy, nz = disp.shape
    bpd, sblk, _ = mortar.shape
    f32 = jnp.float32
    any_spec = pl.BlockSpec(memory_space=pl.ANY)
    vmem = pl.BlockSpec(memory_space=pltpu.VMEM)
    rows = cy + 2 * YB
    rowblk = ngx * bpd
    count = nb * ngx * ngy
    dma = pltpu.SemaphoreType.DMA
    full = pltpu.VMEM((bpd, sblk, nz), f32)
    most = max((comp + 1) * cx * cy, (comp + 1 + 2 * (comp - 1)) * 2 * (cy + cx + 2), count, bpd * sblk,
               3 * bpd * 4 * ngx)
    field = (comp, cx + 2, rows, nz)
    r0, v1, coef, npr = pl.pallas_call(
        functools.partial(kernel, nb, ngx, ngy),
        out_shape=(pltpu.VMEM((comp, cx, cy, nz), f32), pltpu.VMEM((comp, cx, cy, nz), f32), pltpu.VMEM((8, nz), f32),
                   pltpu.VMEM((3, bpd, 1, sblk), f32)),
        in_specs=[any_spec] * 9,
        out_specs=(vmem,) * 4,
        scratch_shapes=[
            pltpu.VMEM((bpd, sblk), f32),
            pltpu.VMEM((bpd, sblk), f32),
            pltpu.SMEM((bpd,), jnp.int32),
            pltpu.SMEM((bpd,), jnp.int32),
            pltpu.VMEM((comp + 1, cx + 2, rows, nz), f32),
            pltpu.VMEM(field, f32),
            pltpu.VMEM(field, f32),
            pltpu.VMEM((3, bpd, 1, sblk), f32),
            pltpu.VMEM((cx, cy, nz), f32),
            pltpu.VMEM((comp, cx, cy, nz), f32),
            pltpu.VMEM((cx, cy, nz), f32),
            pltpu.VMEM((bpd, sblk, sblk), f32),
            pltpu.VMEM((3, ngx, bpd, 1, sblk), f32),
            pltpu.VMEM((3, ngx, 3, bpd, 1, sblk), f32),
            pltpu.VMEM((3, rowblk + 2, 1, sblk), f32),
            full, full, full, full, full, full, full, full,
            pltpu.VMEM((8, 8, nz), f32),
            pltpu.VMEM((cy, nz), f32),
            pltpu.VMEM((count, 1, sblk), f32),
            pltpu.VMEM((most, 1, nz), f32),
            dma((7,)), dma((5,)), dma((3,)), dma((3,)), dma((1,)), dma((2,)), dma((2,)), dma((2, 2)), dma((1,)), dma((2,)),
            dma((2,)),
        ],
        compiler_params=pltpu.CompilerParams(collective_id=0, has_side_effects=True,
                                             vmem_limit_bytes=60 * 1024 * 1024),
        name="newton_step",
    )(disp, force, kappa, sigma, gap0, pressure, mortar, partner, active)
    return pl.pallas_call(
        out_kernel,
        out_shape=(jax.ShapeDtypeStruct(disp.shape, f32), jax.ShapeDtypeStruct(gap0.shape, f32)),
        in_specs=[vmem] * 4,
        out_specs=(any_spec, any_spec),
        scratch_shapes=[pltpu.VMEM((comp, cx, cy, nz), f32), pltpu.VMEM((bpd, sblk), f32), dma((comp + 1,))],
        compiler_params=pltpu.CompilerParams(vmem_limit_bytes=4 * 1024 * 1024),
        name="newton_out",
    )(r0, v1, coef, npr)


def solution(mesh):
    placed = (
        P("body", None, "gx", "gy", None),
        P("body", None, "gx", "gy", None),
        P("body", "gx", "gy", None),
        P("body", "gx", "gy", None),
        P(("gx", "gy"), None),
        P(("gx", "gy"), None),
        P(("gx", "gy"), None, None),
        P(("gx", "gy")),
        P(("gx", "gy")),
    )
    return jax.shard_map(
        on_device,
        mesh=mesh,
        in_specs=placed,
        out_specs=(P("body", None, "gx", "gy", None), P(("gx", "gy"), None)),
        check_vma=False,
    )
```

```python
import functools

import jax
import jax.numpy as jnp
from jax import lax
from jax.experimental import pallas as pl
from jax.experimental.pallas import tpu as pltpu
from jax.sharding import PartitionSpec as P

MESH = pl.DeviceIdType.MESH
YB = 8
CORNERS = tuple((dx, dy) for dx in (-1, 1) for dy in (-1, 1))
ALONG_Y = ((0, -1), (0, 1))
ACROSS_X = CORNERS + ((-1, 0), (1, 0))
FACES_X = ((-1, 0), (1, 0))
DIRS = CORNERS + ALONG_Y + FACES_X
RR, RV, VV, NN, NV, NW, VW, OWN = range(8)


def kernel(nb, ngx, ngy, disp, force, kappa, sigma, gap0_in, press_in, mortar, partner_in, active_in,
           r0_out, v1_out, coef, npr_out,
           gap0, press, partner, active, f0, f1, f2, npr, diag, force_v, sigma_v, mort, s1b, pbuf, ub, base, prs_f, t_f, ex_f, sl_f,
           st_f, gr_f, gv_f, acc, own_ref, final, dummy,
           ls, hr, hs, sr, ss, pr, pq, pn, ps, nps, fin):
    comp, cx, cy, nz = force_v.shape
    bpd, sblk = gap0.shape
    per = sblk // cy
    rowblk = ngx * bpd
    last = comp - 1
    b = lax.axis_index("body")
    gx = lax.axis_index("gx")
    gy = lax.axis_index("gy")
    count = nb * ngx * ngy
    me = (b * ngx + gx) * ngy + gy
    f32 = jnp.float32

    def far(at, k, size):
        if size & (size - 1):
            return lax.rem(at + k, size)
        for bit in (1 << i for i in range(size.bit_length() - 1)):
            if k & bit:
                at = at + bit - 2 * bit * lax.rem(at // bit, 2)
        return at

    def place_of(other):
        return {"body": other // (ngx * ngy), "gx": lax.rem(other // ngy, ngx), "gy": lax.rem(other, ngy)}

    def each_peer(act):
        if count <= 64:
            for k in range(1, count):
                act(k)
        else:
            pl.loop(1, count)(act)

    def exists(dx, dy):
        good = jnp.bool_(True)
        if dx < 0:
            good = good & (gx >= 1)
        if dx > 0:
            good = good & (gx < ngx - 1)
        if dy < 0:
            good = good & (gy >= 1)
        if dy > 0:
            good = good & (gy < ngy - 1)
        return good

    def as_int(flag):
        return flag.astype(jnp.int32)

    nys = as_int(exists(0, -1)) + as_int(exists(0, 1))
    nxs = as_int(exists(-1, 0)) + as_int(exists(1, 0))

    def sides(size):
        return (0,) if size == 1 else (1,) if size == 2 else (1, 2)

    def wait_rows(sem, rows):
        part = dummy.at[pl.ds(0, rows)]
        pltpu.make_async_copy(part, part, sem).wait()

    def wait_halo(sem, comps):
        for a in sides(ngx):
            for c in sides(ngy):
                rows = comps * (a * cy + c * cx + a * c)
                if rows:
                    pl.when((nxs == a) & (nys == c))(lambda: wait_rows(sem, rows))

    barrier = pltpu.get_barrier_semaphore()
    if ngy <= 4:
        expect = jnp.where(b == 1, ngx, 0)
        @pl.when(b == 0)
        def _():
            for k in reversed(range(ngx)):
                pl.semaphore_signal(barrier, inc=1, device_id={"body": 1, "gx": far(gx, k, ngx)},
                                    device_id_type=MESH)
        for dx, dy in DIRS:
            here = exists(dx, dy)
            expect = expect + as_int(here)

            @pl.when(here)
            def _():
                pl.semaphore_signal(barrier, inc=1, device_id={"gx": gx + dx, "gy": gy + dy}, device_id_type=MESH)
    else:
        each_peer(lambda k: pl.semaphore_signal(barrier, inc=1, device_id=place_of(lax.rem(me + k, count)),
                                                device_id_type=MESH))
        expect = count - 1

    inner = (pl.ds(1, cx), pl.ds(YB, cy))
    pltpu.make_async_copy(disp.at[0, last], f0.at[(last,) + inner], ls.at[0]).start()
    pltpu.make_async_copy(disp.at[0, pl.ds(0, last)], f0.at[(pl.ds(0, last),) + inner], ls.at[1]).start()
    pltpu.make_async_copy(kappa.at[0], f0.at[(comp,) + inner], ls.at[1]).start()
    pltpu.make_async_copy(gap0_in, gap0, ls.at[3]).start()
    pltpu.make_async_copy(press_in, press, ls.at[3]).start()
    pltpu.make_async_copy(partner_in, partner, ls.at[4]).start()
    pltpu.make_async_copy(active_in, active, ls.at[5]).start()
    pltpu.make_async_copy(mortar, mort, ls.at[6]).start()
    pltpu.make_async_copy(sigma.at[0], sigma_v, ls.at[2]).start()
    pltpu.make_async_copy(force.at[0], force_v, ls.at[2]).start()

    for side, x in ((-1, 0), (1, cx + 1)):
        @pl.when(jnp.logical_not(exists(side, 0)))
        def _():
            for f in (f0, f1, f2):
                for c in range(f.shape[0]):
                    f[c, x, YB - 1 : YB] = jnp.zeros((1, nz), f32)
                    f[c, x, YB : YB + cy] = jnp.zeros((cy, nz), f32)
                    f[c, x, YB + cy : YB + cy + 1] = jnp.zeros((1, nz), f32)
    for side, y in ((-1, YB - 1), (1, YB + cy)):
        @pl.when(jnp.logical_not(exists(0, side)))
        def _():
            for f in (f0, f1, f2):
                for c in range(f.shape[0]):
                    for x in range(cx + 2):
                        f[c, x, y : y + 1] = jnp.zeros((1, nz), f32)
            for g in range(ngx):
                for k in range(3):
                    for l in range(bpd):
                        pbuf[1 + side, g, k, l] = jnp.zeros((1, sblk), f32)
    for d in range(3):
        for q in (0, rowblk + 1):
            ub[d, q] = jnp.zeros((1, sblk), f32)
    for k in range(8):
        acc[k] = jnp.zeros((8, nz), f32)

    lane = lax.broadcasted_iota(jnp.int32, (sblk, nz), 1)
    eye = lax.broadcasted_iota(jnp.int32, (sblk, nz), 0) == lane
    first_lane = lane == 0
    lane_row = lax.broadcasted_iota(jnp.int32, (cy, nz), 1)
    left_w = jnp.where(lane_row == 0, 0.0, 0.5)
    right_w = jnp.where(lane_row == nz - 1, 0.0, 0.5)
    lane_one = lax.broadcasted_iota(jnp.int32, (1, nz), 1)
    block_of = lax.broadcasted_iota(jnp.int32, (rowblk, sblk), 0)
    block_f = block_of.astype(f32)

    def to_full(row):
        return jnp.broadcast_to(jnp.sum(jnp.where(eye, row, 0.0), axis=1, keepdims=True), (sblk, nz))

    def to_row(full):
        return jnp.sum(jnp.where(eye, full, 0.0), axis=0, keepdims=True)

    def tz(v):
        return v + left_w * pltpu.roll(v, 1, 1) + right_w * pltpu.roll(v, nz - 1, 1)

    def block(f, l):
        return f[last, 1 + l * per : 1 + (l + 1) * per, YB : YB + cy, :].reshape(sblk, nz)

    def first_of(f, l):
        return jnp.broadcast_to(block(f, l)[:, 0:1], (sblk, nz))

    def take_off(f, l, full):
        xs = slice(1 + l * per, 1 + (l + 1) * per)
        f[last, xs, YB : YB + cy, :] = (block(f, l) - jnp.where(first_lane, full, 0.0)).reshape(per, cy, nz)

    def part(delta, size, base_at, src_base):
        if delta == 0:
            return pl.ds(src_base, size), pl.ds(base_at, size)
        if delta < 0:
            return pl.ds(src_base, 1), pl.ds(base_at + size, 1)
        return pl.ds(src_base + size - 1, 1), pl.ds(base_at - 1, 1)

    def halo_send(f, at, size, send_sem, recv_sem, dirs):
        cs = pl.ds(at, size)
        for dx, dy in dirs:
            @pl.when(exists(dx, dy))
            def _():
                sx, tx = part(dx, cx, 1, 1)
                sy, ty = part(dy, cy, YB, YB)
                pltpu.make_async_remote_copy(
                    src_ref=f.at[cs, sx, sy], dst_ref=f.at[cs, tx, ty], send_sem=send_sem, recv_sem=recv_sem,
                    device_id={"gx": gx + dx, "gy": gy + dy}, device_id_type=MESH).start()

    def halo_send_args(dirs):
        for dx, dy in dirs:
            @pl.when(exists(dx, dy))
            def _():
                sx, tx = part(dx, cx, 1, 0)
                sy, ty = part(dy, cy, YB, 0)
                for src, dst in ((disp.at[0, :, sx, sy], f0.at[pl.ds(0, comp), tx, ty]),
                                 (kappa.at[:, sx, sy], f0.at[pl.ds(comp, 1), tx, ty])):
                    pltpu.make_async_remote_copy(
                        src_ref=src, dst_ref=dst, send_sem=hs.at[0], recv_sem=hr.at[0],
                        device_id={"gx": gx + dx, "gy": gy + dy}, device_id_type=MESH).start()

    def surf_send(r):
        for k in reversed(range(ngx)):
            pltpu.make_async_remote_copy(
                src_ref=s1b.at[r, gx], dst_ref=s1b.at[r, gx], send_sem=ss.at[0], recv_sem=sr.at[r],
                device_id={"body": 0, "gx": far(gx, k, ngx)}, device_id_type=MESH).start()

    def surface_rows(f, r):
        for l in range(bpd):
            s1b[r, gx, l] = to_row(first_of(f, l))

    def pulled_send(first, size, r):
        ks = pl.ds(first, size)

        def go(bo, g, sem):
            pltpu.make_async_remote_copy(
                src_ref=pbuf.at[1, gx, ks], dst_ref=pbuf.at[1, gx, ks], send_sem=ps.at[0], recv_sem=sem,
                device_id={"body": bo, "gx": g}, device_id_type=MESH).start()
        go(1, gx, pq.at[r])
        for k in reversed(range(1, ngx)):
            go(1, far(gx, k, ngx), pr.at[r])
            go(0, far(gx, k, ngx), pr.at[r])

    def pass_on(r, first, size):
        ks = pl.ds(first, size)
        wait_rows(pq.at[r], size * bpd)
        for s in (-1, 1):
            @pl.when(exists(0, s))
            def _():
                for k in reversed(range(ngx)):
                    pltpu.make_async_remote_copy(
                        src_ref=pbuf.at[1, gx, ks], dst_ref=pbuf.at[1 - s, gx, ks], send_sem=ps.at[0],
                        recv_sem=pn.at[r, (1 - s) // 2], device_id={"gx": far(gx, k, ngx), "gy": gy + s},
                        device_id_type=MESH).start()

    def expand(d, k):
        u = jnp.zeros((rowblk, sblk), f32)
        for g in range(ngx):
            for l in range(bpd):
                u = u + jnp.where(block_f == pbuf[d, g, 1, l], pbuf[d, g, k, l], 0.0)
        return u

    def ring_fix(f, r, k, size):
        if ngx > 1:
            wait_rows(pr.at[r], (ngx - 1) * size * bpd)
        ub[1, 1 : 1 + rowblk] = expand(1, k).reshape(rowblk, 1, sblk)

        def row(d, j):
            return ub[d, gx * bpd + j]

        for l in range(bpd):
            take_off(f, l, to_full(row(1, 1 + l)))
        for j, x, at in ((0, 0, sblk - cy), (bpd + 1, cx + 1, 0)):
            col = jnp.sum(jnp.where(eye[at : at + cy], row(1, j), 0.0), axis=1, keepdims=True)
            f[last, x, YB : YB + cy, :] = f[last, x, YB : YB + cy, :] - jnp.where(lane_row == 0, col, 0.0)
        if r == 0:
            pass_on(1, 2, 1)
        for d, y, off in ((0, YB - 1, cy - 1), (2, YB + cy, 0)):
            pl.when(exists(0, d - 1))(lambda: wait_rows(pn.at[r, d // 2], ngx * size * bpd))
            ub[d, 1 : 1 + rowblk] = expand(d, k).reshape(rowblk, 1, sblk)
            for xi in range(cx + 2):
                j = (xi - 1 + per) // per
                at = ((xi - 1 + per) % per) * cy + off
                val = pltpu.roll(row(d, j), (nz - at) % nz, 1)
                f[last, xi, y : y + 1, :] = f[last, xi, y : y + 1, :] - jnp.where(lane_one == 0, val, 0.0)

    def planes(f, c, emit, first, stop):
        window = []
        for x in range(first, stop + 2):
            kap = [f0[comp, x, YB + s : YB + s + cy, :] for s in (-1, 0, 1)]
            val = [f[c, x, YB + s : YB + s + cy, :] for s in (-1, 0, 1)]
            window.append((val[1] + 0.5 * (val[0] + val[2]),
                           kap[1] * val[1] + 0.5 * (kap[0] * val[0] + kap[2] * val[2])))
            if len(window) >= 3:
                p = window[-2][0] + 0.5 * (window[-3][0] + window[-1][0])
                q = window[-2][1] + 0.5 * (window[-3][1] + window[-1][1])
                k0 = f0[comp, x - 1, YB : YB + cy, :]
                v0 = f[c, x - 1, YB : YB + cy, :]
                emit(c, x - 2, diag[x - 2] * v0 - k0 * tz(p) - tz(q))

    def apply(f, c, emit):
        planes(f, c, emit, 0, cx)

    def edges(f, c, emit):
        planes(f, c, emit, 0, 1)
        planes(f, c, emit, cx - 1, cx)

    def inside(f, c, emit):
        planes(f, c, emit, 1, cx - 1)

    def make_diag():
        window = []
        for x in range(cx + 2):
            kap = [f0[comp, x, YB + s : YB + s + cy, :] for s in (-1, 0, 1)]
            window.append(kap[1] + 0.5 * (kap[0] + kap[2]))
            if x >= 2:
                p = window[x - 1] + 0.5 * (window[x - 2] + window[x])
                diag[x - 2] = sigma_v[x - 2] + 8.0 * f0[comp, x - 1, YB : YB + cy, :] + tz(p)

    def emit_rhs(c, x, val):
        f1[c, 1 + x, YB : YB + cy, :] = force_v[c, x] - val

    def emit_v1(c, x, val):
        f2[c, 1 + x, YB : YB + cy, :] = val

    def traction(x):
        rows = slice((x % per) * cy, (x % per + 1) * cy)
        return jnp.where(lane_row == 0, t_f[x // per, rows, :], 0.0)

    def emit_rhs_t(c, x, val):
        f1[c, 1 + x, YB : YB + cy, :] = force_v[c, x] - val - traction(x)

    def emit_v1_t(c, x, val):
        f2[c, 1 + x, YB : YB + cy, :] = val - traction(x)

    def r0_of(c, x):
        return f1[c, 1 + x, YB : YB + cy, :]

    def v1_of(c, x):
        return f2[c, 1 + x, YB : YB + cy, :]

    def fold(v):
        return jnp.sum(v.reshape(cy // 8, 8, nz), axis=0)

    def gather(c, wanted, fields):
        sums = {}
        for x in range(cx):
            for k, (left, right) in wanted.items():
                term = fold(fields(x)[left] * fields(x)[right])
                sums[k] = sums[k] + term if k in sums else term
        for k, v in sums.items():
            acc[k] = acc[k] + v

    def dots(c):
        gather(c, {RR: (0, 0), RV: (0, 1), VV: (1, 1)}, lambda x: (r0_of(c, x), v1_of(c, x)))

    def total(v):
        return jnp.sum(jnp.sum(v, axis=0, keepdims=True), axis=1, keepdims=True)

    def choose_own():
        rv, vv = total(acc[RV]), total(acc[VV])
        own = jnp.where(vv > 0.0, rv / jnp.where(vv > 0.0, vv, 1.0), 0.0)
        own_ref[...] = jnp.broadcast_to(own, (cy, nz))

    def near_dots(c):
        own = own_ref[...]
        gather(c, {NN: (0, 0), NV: (0, 1)}, lambda x: (r0_of(c, x) - own * v1_of(c, x), v1_of(c, x)))

    def image_dots(c, more):
        own = own_ref[...]
        sums = {}

        def emit(c, x, val):
            v = v1_of(c, x)
            r = r0_of(c, x)
            near = r - own * v
            terms = {NW: near * val, VW: v * val}
            if more:
                terms.update({RV: r * v, VV: v * v, NN: near * near, NV: near * v})
            for k, t in terms.items():
                sums[k] = sums[k] + fold(t) if k in sums else fold(t)
        apply(f2, c, emit)
        for k, v in sums.items():
            acc[k] = acc[k] + v

    def first_comps(act):
        for c in range(last):
            act(c)

    def gap_of(l, s1):
        picked = jnp.sum(jnp.where(block_of == partner[l], s1, 0.0), axis=0, keepdims=True)
        return base[l] - jnp.broadcast_to(jnp.sum(mort[l] * picked, axis=1, keepdims=True), (sblk, nz))

    def pull(l, k, t):
        pbuf[1, gx, k, l] = jnp.sum(mort[l] * t, axis=0, keepdims=True)

    def surf_rows(r):
        return s1b[r].reshape(rowblk, sblk)

    def send_final():
        sub = lax.broadcasted_iota(jnp.int32, (8, nz), 0)
        stack = jnp.zeros((8, nz), f32)
        for k in range(OWN):
            stack = jnp.where(sub == k, jnp.broadcast_to(jnp.sum(acc[k], axis=0, keepdims=True), (8, nz)), stack)
        lanes = lax.broadcasted_iota(jnp.int32, (8, nz), 1)
        stack = jnp.where((sub == OWN) & (lanes == 0), own_ref[0:8, :], stack)
        final[me] = jnp.sum(jnp.where(sub == lanes, jnp.sum(stack, axis=1, keepdims=True), 0.0), axis=0, keepdims=True)

        def go(place):
            pltpu.make_async_remote_copy(
                src_ref=final.at[me], dst_ref=final.at[me], send_sem=fin.at[0], recv_sem=fin.at[1],
                device_id=place, device_id_type=MESH).start()
        if count <= 64:
            for kx in reversed(range(ngx)):
                for ky in reversed(range(ngy)):
                    for kb in reversed(range(nb)):
                        if kx or ky or kb:
                            go({"body": far(b, kb, nb), "gx": far(gx, kx, ngx), "gy": far(gy, ky, ngy)})
        else:
            each_peer(lambda k: go(place_of(lax.rem(me + k, count))))

    def first_surface():
        wait_rows(ls.at[0], cx * cy)
        surface_rows(f0, 0)

    pl.when((b == 1) & (gx < ngx - 1))(first_surface)
    pl.semaphore_wait(barrier, expect)
    halo_send_args(CORNERS + ALONG_Y)

    @pl.when(b == 1)
    def _():
        pl.when(gx == ngx - 1)(first_surface)
        surf_send(0)

    halo_send_args(FACES_X)

    @pl.when(b == 1)
    def _():
        wait_rows(ls.at[1], comp * cx * cy)
        wait_rows(ls.at[2], (comp + 1) * cx * cy)
        wait_halo(hr.at[0], comp + 1)
        make_diag()
        first_comps(lambda c: edges(f0, c, emit_rhs))
        halo_send(f1, 0, last, hs.at[0], hr.at[1], ACROSS_X)
        edges(f0, last, emit_rhs)
        halo_send(f1, last, 1, hs.at[1], hr.at[2], ACROSS_X)
        inside(f0, last, emit_rhs)
        surface_rows(f1, 1)
        surf_send(1)
        halo_send(f1, last, 1, hs.at[1], hr.at[2], ALONG_Y)
        pass_on(0, 0, 2)
        first_comps(lambda c: inside(f0, c, emit_rhs))
        halo_send(f1, 0, last, hs.at[0], hr.at[1], ALONG_Y)

        wait_halo(hr.at[1], last)
        first_comps(lambda c: edges(f1, c, emit_v1))
        halo_send(f2, 0, last, hs.at[0], hr.at[3], ACROSS_X)
        first_comps(lambda c: inside(f1, c, emit_v1))
        halo_send(f2, 0, last, hs.at[0], hr.at[3], ALONG_Y)
        wait_halo(hs.at[1], 1)
        wait_halo(hr.at[2], 1)
        ring_fix(f1, 0, 0, 2)
        edges(f1, last, emit_v1)
        halo_send(f2, last, 1, hs.at[2], hr.at[4], ACROSS_X)
        inside(f1, last, emit_v1)
        surface_rows(f2, 2)
        surf_send(2)
        halo_send(f2, last, 1, hs.at[2], hr.at[4], ALONG_Y)
        first_comps(dots)
        choose_own()
        first_comps(near_dots)
        gather(last, {RR: (0, 0)}, lambda x: (r0_of(last, x),))

        wait_halo(hr.at[3], last)
        first_comps(lambda c: image_dots(c, False))
        wait_halo(hs.at[2], 1)
        wait_halo(hr.at[4], 1)
        ring_fix(f2, 1, 2, 1)
        image_dots(last, True)
        send_final()

    @pl.when(b == 0)
    def _():
        for k in range(4):
            sem, rows = ((ls.at[0], cx * cy), (ls.at[3], 2 * bpd), (ls.at[6], bpd * sblk), (ls.at[1], comp * cx * cy))[k]
            wait_rows(sem, rows)
        pltpu.make_async_copy(partner_in, partner, ls.at[4]).wait()
        pltpu.make_async_copy(active_in, active, ls.at[5]).wait()
        for l in range(bpd):
            base[l] = to_full(gap0[l : l + 1, :]) - first_of(f0, l)
            prs_f[l] = to_full(press[l : l + 1, :])
            pbuf[1, gx, 1, l] = jnp.full((1, sblk), partner[l].astype(f32))
        wait_rows(sr.at[0], ngx * bpd)
        s1 = surf_rows(0)
        for l in range(bpd):
            gap = gap_of(l, s1)
            prs = prs_f[l]
            radius = jnp.sqrt(gap * gap + prs * prs + 0.01)
            per_radius = 1.0 / radius
            per_divisor = 1.0 / ((1.0 - prs * per_radius) + 0.5)
            flag = active[l].astype(f32)
            excess = (gap + prs - radius) * per_divisor
            slope = (1.0 - gap * per_radius) * per_divisor
            t = flag * (prs - excess)
            pull(l, 0, t)
            t_f[l] = t
            ex_f[l] = excess
            sl_f[l] = slope
            st_f[l] = flag * slope
        pulled_send(0, 2, 0)
        wait_rows(ls.at[2], (comp + 1) * cx * cy)
        wait_halo(hr.at[0], comp + 1)
        make_diag()
        first_comps(lambda c: edges(f0, c, emit_rhs))
        halo_send(f1, 0, last, hs.at[0], hr.at[1], ACROSS_X)
        edges(f0, last, emit_rhs_t)
        halo_send(f1, last, 1, hs.at[1], hr.at[2], ACROSS_X)
        first_comps(lambda c: inside(f0, c, emit_rhs))
        halo_send(f1, 0, last, hs.at[0], hr.at[1], ALONG_Y)
        inside(f0, last, emit_rhs_t)
        halo_send(f1, last, 1, hs.at[1], hr.at[2], ALONG_Y)
        for l in range(bpd):
            base[l] = -first_of(f1, l)

        wait_rows(sr.at[1], ngx * bpd)
        if ngx > 1:
            wait_rows(pr.at[0], (ngx - 1) * 2 * bpd)
        s1 = surf_rows(1) - expand(1, 0)
        for l in range(bpd):
            gap = gap_of(l, s1)
            t = st_f[l] * gap
            pull(l, 2, t)
            t_f[l] = t
            gr_f[l] = gap
        pulled_send(2, 1, 1)
        wait_halo(hr.at[1], last)
        first_comps(lambda c: edges(f1, c, emit_v1))
        halo_send(f2, 0, last, hs.at[0], hr.at[3], ACROSS_X)
        wait_halo(hr.at[2], 1)
        edges(f1, last, emit_v1_t)
        halo_send(f2, last, 1, hs.at[2], hr.at[4], ACROSS_X)
        first_comps(lambda c: inside(f1, c, emit_v1))
        halo_send(f2, 0, last, hs.at[0], hr.at[3], ALONG_Y)
        inside(f1, last, emit_v1_t)
        halo_send(f2, last, 1, hs.at[2], hr.at[4], ALONG_Y)
        for l in range(bpd):
            base[l] = -first_of(f2, l)
        first_comps(dots)
        choose_own()
        dots(last)
        pl.loop(0, comp)(near_dots)
        wait_halo(hr.at[3], last)
        first_comps(lambda c: image_dots(c, False))
        wait_halo(hr.at[4], 1)
        image_dots(last, False)

        wait_rows(sr.at[2], ngx * bpd)
        if ngx > 1:
            wait_rows(pr.at[1], (ngx - 1) * bpd)
        s1 = surf_rows(2) - expand(1, 2)
        own = own_ref[0:1, :]
        for l in range(bpd):
            gap = gap_of(l, s1)
            gv_f[l] = gap
            weighted = st_f[l] * gap
            for k, left in ((NW, gr_f[l] - own * gap), (VW, gap)):
                row = jnp.sum(weighted * left, axis=0, keepdims=True)
                acc[k, 0:1] = acc[k, 0:1] + jnp.where(lane_one == 0, row, 0.0)
        send_final()
        for l in range(bpd):
            flag = active[l].astype(f32)
            npr[0, l] = flag * (press[l : l + 1, :] - to_row(ex_f[l]))
            npr[1, l] = flag * to_row(sl_f[l] * gr_f[l])
            npr[2, l] = flag * to_row(sl_f[l] * gv_f[l])
        pltpu.make_async_remote_copy(src_ref=npr, dst_ref=npr, send_sem=nps.at[0], recv_sem=nps.at[1],
                                     device_id={"body": 1}, device_id_type=MESH).start()

    @pl.when(b == 1)
    def _():
        wait_rows(ls.at[3], 2 * bpd)
        wait_rows(ls.at[6], bpd * sblk)
        pltpu.make_async_copy(partner_in, partner, ls.at[4]).wait()
        pltpu.make_async_copy(active_in, active, ls.at[5]).wait()
        wait_rows(ss.at[0], 3 * ngx * bpd)
        for c in sides(ngy):
            if c:
                pl.when(nys == c)(lambda: wait_rows(ps.at[0], 3 * bpd * c * ngx))
        wait_rows(nps.at[1], 3 * bpd)

    @pl.when(b == 0)
    def _():
        wait_rows(ps.at[0], 3 * bpd * (2 * ngx - 1))
        wait_halo(hs.at[1], 1)
        wait_halo(hs.at[2], 1)
        wait_rows(nps.at[0], 3 * bpd)

    wait_halo(hs.at[0], comp + 1 + 2 * last)
    wait_rows(fin.at[0], count - 1)
    for c in range(comp):
        for x in range(cx):
            r0_out[c, x] = r0_of(c, x)
            v1_out[c, x] = v1_of(c, x)
    npr_out[...] = npr[...]

    wait_rows(fin.at[1], count - 1)
    table = final[...].reshape(count, sblk)
    lanes = lax.broadcasted_iota(jnp.int32, (count, sblk), 1)
    sums = jnp.sum(table, axis=0, keepdims=True)
    norm0 = sums[:, RR : RR + 1]
    product0 = sums[:, RV : RV + 1]
    alpha0 = norm0 / product0
    per_norm0 = 1.0 / norm0
    delta = alpha0 - table[:, OWN : OWN + 1]

    def pick(weights):
        w = jnp.zeros((count, sblk), f32)
        for k, v in weights:
            w = jnp.where(lanes == k, v, w)
        return total(w * table)

    norm1 = pick(((NN, 1.0), (NV, -2.0 * delta), (VV, delta * delta)))
    product1 = pick(((NV, 1.0), (VV, -delta), (NW, -alpha0), (VW, alpha0 * delta)))
    ratio = norm1 * per_norm0
    alpha1 = norm1 / (product1 - ratio * (ratio * product0))
    coef[0:1, :] = jnp.broadcast_to(alpha0 + alpha1 * (1.0 + ratio), (1, nz))
    coef[1:2, :] = jnp.broadcast_to(-alpha1 * alpha0, (1, nz))


def out_kernel(r0, v1, coef, npr, inc, new_press, buf, rows, sems):
    comp, cx, cy, nz = buf.shape
    bpd = rows.shape[0]
    cr, cv = coef[0:1, :], coef[1:2, :]
    copies = []
    for l in range(bpd):
        rows[l : l + 1, :] = npr[0, l] - (cr * npr[1, l] + cv * npr[2, l])
    copies.append(pltpu.make_async_copy(rows, new_press, sems.at[comp]))
    copies[-1].start()
    for c in range(comp):
        for x in range(cx):
            buf[c, x] = cr * r0[c, x] + cv * v1[c, x]
        copies.append(pltpu.make_async_copy(buf.at[c], inc.at[0, c], sems.at[c]))
        copies[-1].start()
    for copy in copies:
        copy.wait()


def on_device(disp, force, kappa, sigma, gap0, pressure, mortar, partner, active):
    nb, ngx, ngy = (lax.axis_size(a) for a in ("body", "gx", "gy"))
    _, comp, cx, cy, nz = disp.shape
    bpd, sblk, _ = mortar.shape
    f32 = jnp.float32
    any_spec = pl.BlockSpec(memory_space=pl.ANY)
    vmem = pl.BlockSpec(memory_space=pltpu.VMEM)
    rows = cy + 2 * YB
    rowblk = ngx * bpd
    count = nb * ngx * ngy
    dma = pltpu.SemaphoreType.DMA
    full = pltpu.VMEM((bpd, sblk, nz), f32)
    most = max((comp + 1) * cx * cy, (comp + 1 + 2 * (comp - 1)) * 2 * (cy + cx + 2), count, bpd * sblk,
               3 * bpd * 4 * ngx)
    field = (comp, cx + 2, rows, nz)
    r0, v1, coef, npr = pl.pallas_call(
        functools.partial(kernel, nb, ngx, ngy),
        out_shape=(pltpu.VMEM((comp, cx, cy, nz), f32), pltpu.VMEM((comp, cx, cy, nz), f32), pltpu.VMEM((8, nz), f32),
                   pltpu.VMEM((3, bpd, 1, sblk), f32)),
        in_specs=[any_spec] * 9,
        out_specs=(vmem,) * 4,
        scratch_shapes=[
            pltpu.VMEM((bpd, sblk), f32),
            pltpu.VMEM((bpd, sblk), f32),
            pltpu.SMEM((bpd,), jnp.int32),
            pltpu.SMEM((bpd,), jnp.int32),
            pltpu.VMEM((comp + 1, cx + 2, rows, nz), f32),
            pltpu.VMEM(field, f32),
            pltpu.VMEM(field, f32),
            pltpu.VMEM((3, bpd, 1, sblk), f32),
            pltpu.VMEM((cx, cy, nz), f32),
            pltpu.VMEM((comp, cx, cy, nz), f32),
            pltpu.VMEM((cx, cy, nz), f32),
            pltpu.VMEM((bpd, sblk, sblk), f32),
            pltpu.VMEM((3, ngx, bpd, 1, sblk), f32),
            pltpu.VMEM((3, ngx, 3, bpd, 1, sblk), f32),
            pltpu.VMEM((3, rowblk + 2, 1, sblk), f32),
            full, full, full, full, full, full, full, full,
            pltpu.VMEM((8, 8, nz), f32),
            pltpu.VMEM((cy, nz), f32),
            pltpu.VMEM((count, 1, sblk), f32),
            pltpu.VMEM((most, 1, nz), f32),
            dma((7,)), dma((5,)), dma((3,)), dma((3,)), dma((1,)), dma((2,)), dma((2,)), dma((2, 2)), dma((1,)), dma((2,)),
            dma((2,)),
        ],
        compiler_params=pltpu.CompilerParams(collective_id=0, has_side_effects=True,
                                             vmem_limit_bytes=60 * 1024 * 1024),
        name="newton_step",
    )(disp, force, kappa, sigma, gap0, pressure, mortar, partner, active)
    return pl.pallas_call(
        out_kernel,
        out_shape=(jax.ShapeDtypeStruct(disp.shape, f32), jax.ShapeDtypeStruct(gap0.shape, f32)),
        in_specs=[vmem] * 4,
        out_specs=(any_spec, any_spec),
        scratch_shapes=[pltpu.VMEM((comp, cx, cy, nz), f32), pltpu.VMEM((bpd, sblk), f32), dma((comp + 1,))],
        compiler_params=pltpu.CompilerParams(vmem_limit_bytes=4 * 1024 * 1024),
        name="newton_out",
    )(r0, v1, coef, npr)


def solution(mesh):
    placed = (
        P("body", None, "gx", "gy", None),
        P("body", None, "gx", "gy", None),
        P("body", "gx", "gy", None),
        P("body", "gx", "gy", None),
        P(("gx", "gy"), None),
        P(("gx", "gy"), None),
        P(("gx", "gy"), None, None),
        P(("gx", "gy")),
        P(("gx", "gy")),
    )
    return jax.shard_map(
        on_device,
        mesh=mesh,
        in_specs=placed,
        out_specs=(P("body", None, "gx", "gy", None), P(("gx", "gy"), None)),
        check_vma=False,
    )
```
